32 devices in a mesh: clip: 16 (over z, x, core), seq: 2 (over y).
Axes of the slice: x: 2, y: 2, z: 4, core: 2. Of those that a mesh axis runs over, the one named last changes fastest.
Arguments:
- frames: float32 [16, 1024, 768], P('clip', 'seq'), may hold values from -6 to 6
- cotangent: float32 [16, 1024, 768], P('clip', 'seq'), may hold values from -6 to 6
- first_gain: float32 [2, 768], P(None, ('clip', 'seq')), may hold values from 0.5 to 1.5
- first_shift: float32 [2, 768], P(None, ('clip', 'seq')), may hold values from -2 to 2
- mixing_weight: float32 [2, 768, 2304], P(None, ('clip', 'seq')), may hold values from -0.3125 to 0.3125
- mixing_bias: float32 [2, 1536], P(None, ('clip', 'seq')), may hold values from -2 to 2
- output_weight: float32 [2, 768, 768], P(None, ('clip', 'seq')), may hold values from -0.625 to 0.625
- output_bias: float32 [2, 768], P(None, ('clip', 'seq')), may hold values from -2 to 2
- second_gain: float32 [2, 768], P(None, ('clip', 'seq')), may hold values from 0.5 to 1.5
- second_shift: float32 [2, 768], P(None, ('clip', 'seq')), may hold values from -2 to 2
- up_weight: float32 [2, 768, 3072], P(None, ('clip', 'seq')), may hold values from -0.21875 to 0.21875
- up_bias: float32 [2, 3072], P(None, ('clip', 'seq')), may hold values from -3 to 3
- down_weight: float32 [2, 3072, 768], P(None, ('clip', 'seq')), may hold values from -0.15625 to 0.15625
- down_bias: float32 [2, 768], P(None, ('clip', 'seq')), may hold values from -2 to 2
Outputs:
- activations: float32 [16, 1024, 768], P('clip', 'seq')
- input_grad: float32 [16, 1024, 768], P('clip', 'seq')
- first_gain_grad: float32 [2, 768], P(None, ('clip', 'seq'))
- first_shift_grad: float32 [2, 768], P(None, ('clip', 'seq'))
- mixing_weight_grad: float32 [2, 768, 2304], P(None, ('clip', 'seq'))
- mixing_bias_grad: float32 [2, 1536], P(None, ('clip', 'seq'))
- output_weight_grad: float32 [2, 768, 768], P(None, ('clip', 'seq'))
- output_bias_grad: float32 [2, 768], P(None, ('clip', 'seq'))
- second_gain_grad: float32 [2, 768], P(None, ('clip', 'seq'))
- second_shift_grad: float32 [2, 768], P(None, ('clip', 'seq'))
- up_weight_grad: float32 [2, 768, 3072], P(None, ('clip', 'seq'))
- up_bias_grad: float32 [2, 3072], P(None, ('clip', 'seq'))
- down_weight_grad: float32 [2, 3072, 768], P(None, ('clip', 'seq'))
- down_bias_grad: float32 [2, 768], P(None, ('clip', 'seq'))
The draws below stay inside these ranges and needn't reach their ends.
All inputs are finite; a program needn't handle non-finite values.
Results may differ from the reference program's by a relative error of at most 0.017.
The reference program's roundings to bfloat16 on the way count: a program that leaves them out, or rounds other values in their place, can miss the bound.
Values may be sent and summed in bfloat16 or wider, within the bound.
No kernel may reach another device: no remote copies, remote signals or barrier semaphores. Data moves between devices by JAX's collectives and lax.ppermute only.
A program may use at most 320 MiB of HBM per device.

```python
import math
import jax
import jax.numpy as jnp
from jax import lax

D = 768
HEAD_DIM = 64
FF = 3072
LAYERS = 2
LENGTH = 1024
BATCH = 16


def level_of(stream_key, shape, shards, least, top_value):
    factor_of = 1.0
    for position, parts in shards:
        steps = jax.random.uniform(jax.random.fold_in(jax.random.fold_in(stream_key, 6), position), (parts,), jnp.float32, least / len(shards), top_value / len(shards))
        factor_of = factor_of * jnp.repeat(jnp.exp(steps), shape[position] // parts).reshape((-1,) + (1,) * (len(shape) - 1 - position))
    return factor_of


def noise(own_key, dims, deviation, bound, cuts=(), held_as=jnp.bfloat16):
    values = jax.random.normal(own_key, dims, jnp.float32) * deviation
    if len(cuts) > 0:
        values = level_of(own_key, dims, cuts, -0.22, 0.18) * values
    return jnp.clip(values, min=-bound, max=bound).astype(held_as)


def setup_inputs(seed: int = 0) -> dict:
    key_list = jax.random.split(jax.random.key(seed), 15)
    frames = noise(key_list[0], (BATCH, LENGTH, D), 1.0, 6.0, ((0, 16), (1, 2)), jnp.float32)
    cotangent = noise(key_list[1], (BATCH, LENGTH, D), 1.0, 6.0, ((0, 16), (1, 2)), jnp.float32)
    first_gain = jnp.clip(1.0 + 0.1 * jax.random.normal(key_list[2], (LAYERS, D), jnp.float32), 0.5, 1.5)
    first_shift = noise(key_list[3], (LAYERS, D), 0.3, 2.0, ((1, 32),), jnp.float32)
    mixing_weight = noise(key_list[4], (LAYERS, D, 3 * D), (D // 2) ** -0.5, 0.3125, ((1, 32),), jnp.float32)
    mixing_bias = noise(key_list[5], (LAYERS, 2 * D), 0.3, 2.0, ((1, 32),), jnp.float32)
    output_weight = noise(key_list[6], (LAYERS, D, D), (D // 8) ** -0.5, 0.625, ((1, 32),), jnp.float32)
    output_bias = noise(key_list[7], (LAYERS, D), 0.3, 2.0, ((1, 32),), jnp.float32)
    second_gain = jnp.clip(1.0 + 0.1 * jax.random.normal(key_list[8], (LAYERS, D), jnp.float32), 0.5, 1.5)
    second_shift = noise(key_list[9], (LAYERS, D), 0.3, 2.0, ((1, 32),), jnp.float32)
    up_weight = noise(key_list[10], (LAYERS, D, FF), D ** -0.5, 0.21875, ((1, 32),), jnp.float32)
    up_bias = noise(key_list[11], (LAYERS, FF), 0.5, 3.0, ((1, 32),), jnp.float32)
    down_weight = noise(key_list[12], (LAYERS, FF, D), (FF // 2) ** -0.5, 0.15625, ((1, 32),), jnp.float32)
    down_bias = noise(key_list[13], (LAYERS, D), 0.3, 2.0, ((1, 32),), jnp.float32)
    return dict(frames=frames, cotangent=cotangent, first_gain=first_gain, first_shift=first_shift, mixing_weight=mixing_weight, mixing_bias=mixing_bias, output_weight=output_weight, output_bias=output_bias, second_gain=second_gain, second_shift=second_shift, up_weight=up_weight, up_bias=up_bias, down_weight=down_weight, down_bias=down_bias)


@jax.custom_vjp
def low(v):
    return lax.optimization_barrier(v.astype(jnp.bfloat16)).astype(jnp.float32)

@jax.custom_vjp
def low_back(v):
    return v

def low_keep(v):
    return (low(v), None)

def low_pass(kept, grad):
    return (grad,)

def back_keep(v):
    return (v, None)

def back_low(kept, grad):
    return (low(grad),)
low.defvjp(low_keep, low_pass)
low_back.defvjp(back_keep, back_low)

def layer_norm(rows, gain, shift):
    center = lax.optimization_barrier(jnp.mean(rows, axis=-1, keepdims=True))
    spread = rows - center
    variance = lax.optimization_barrier(jnp.mean(spread * spread, axis=-1, keepdims=True))
    return spread * lax.rsqrt(variance + 1e-05) * gain + shift

def product(left, right):
    return jnp.einsum('bfk,kn->bfn', left, right, precision=lax.Precision.HIGHEST)

def encoder_layer(hidden, layer_params):
    first_gain, first_shift, mixing_weight, mixing_bias, output_weight, output_bias, second_gain, second_shift, up_weight, up_bias, down_weight, down_bias = [low(array) for array in layer_params]
    batch, length, width = hidden.shape
    normed = low(layer_norm(hidden, first_gain, first_shift))
    mixed = product(normed, mixing_weight)
    query = low(low_back(mixed[:, :, :width] + mixing_bias[:width]))
    keys = low(low_back(mixed[:, :, width:2 * width]))
    values = low(low_back(mixed[:, :, 2 * width:] + mixing_bias[width:]))
    split = (batch, length, width // HEAD_DIM, HEAD_DIM)
    scores = jnp.einsum('bfhd,blhd->bhfl', query.reshape(split), keys.reshape(split), precision=lax.Precision.HIGHEST) * HEAD_DIM ** (-0.5)
    probs = low(jax.nn.softmax(low_back(scores), axis=-1))
    attended = jnp.einsum('bhfl,blhd->bfhd', probs, values.reshape(split), precision=lax.Precision.HIGHEST).reshape(batch, length, width)
    attended = low(low_back(attended))
    middle = hidden + low_back(product(attended, output_weight) + output_bias)
    normed_two = low(layer_norm(middle, second_gain, second_shift))
    before = low_back(product(normed_two, up_weight) + up_bias)
    active = low(jax.nn.gelu(before, approximate=False))
    return middle + low_back(product(active, down_weight) + down_bias)

def forward(hidden, params):
    for layer in range(LAYERS):
        hidden = encoder_layer(hidden, [array[layer] for array in params])
    return hidden

def add_trees(left, right):
    return jax.tree.map(jnp.add, left, right)

def reference(frames, cotangent, first_gain, first_shift, mixing_weight, mixing_bias, output_weight, output_bias, second_gain, second_shift, up_weight, up_bias, down_weight, down_bias):
    params = (first_gain, first_shift, mixing_weight, mixing_bias, output_weight, output_bias, second_gain, second_shift, up_weight, up_bias, down_weight, down_bias)
    batch = frames.shape[0]
    group = math.gcd(batch, max(1, 4096 // LENGTH))
    grouped = (batch // group, group, LENGTH, frames.shape[2])

    def step(totals, pair):
        block_frames, block_cotangent = pair
        result, pullback = jax.vjp(forward, block_frames, params)
        grad_frames, grad_params = pullback(block_cotangent)
        return (add_trees(totals, grad_params), (result, grad_frames))
    totals, (results, grads) = lax.scan(step, jax.tree.map(jnp.zeros_like, params), (frames.reshape(grouped), cotangent.reshape(grouped)))
    return (results.reshape(frames.shape), grads.reshape(frames.shape), totals[0], totals[1], totals[2], totals[3], totals[4], totals[5], totals[6], totals[7], totals[8], totals[9], totals[10], totals[11])
```

```python
import functools
import math

import jax
import jax.numpy as jnp
from jax import lax
from jax.experimental import pallas as pl
from jax.experimental.pallas import tpu as pltpu
from jax.sharding import PartitionSpec as P

HEAD_DIM = 64
LAYERS = 2
EPSILON = 1e-05
AXES = ("clip", "seq")
LOG2_SCALE = HEAD_DIM ** (-0.5) * math.log2(math.e)
VMEM_BYTES = 56 * 1024 * 1024


class Grid:
    def __init__(self):
        clips, self.seq_size = lax.axis_size("clip"), lax.axis_size("seq")
        self.outer_size = clips // 4
        self.owners = clips * self.seq_size
        self.sizes = (self.outer_size, 2, 2, self.seq_size)
        self.strides = (4 * self.seq_size, 2 * self.seq_size, self.seq_size, 1)

    def digits(self):
        clip, seq = lax.axis_index("clip"), lax.axis_index("seq")
        return (clip // 4, (clip // 2) % 2, clip % 2, seq)

    def shift(self, array, axis, amount):
        size, stride = self.sizes[axis], self.strides[axis]
        pairs = []
        for place in range(self.owners):
            digit = (place // stride) % size
            pairs.append((place, place + ((digit + amount) % size - digit) * stride))
        return lax.ppermute(array, AXES, pairs)


OUTER, CROSS, CORE, SEQ = 0, 1, 2, 3


def place_kernel(grid, steps, splits, *refs):
    count = len(steps)
    pieces, outs, sem = refs[:count], refs[count : count + len(splits)], refs[-1]
    outer, cross, core, seq = grid.digits()
    copies = []
    for piece, step in zip(pieces, steps):
        for back in range(grid.outer_size):
            place = (lax.rem(outer + grid.outer_size - back, grid.outer_size)) * 2
            place = (place + lax.rem(cross + 2 - step[CROSS], 2)) * 2
            place = (place + lax.rem(core + 2 - step[CORE], 2)) * grid.seq_size
            place = place + lax.rem(seq + grid.seq_size - step[SEQ], grid.seq_size)
            for out, (start, stop) in zip(outs, splits):
                source = piece.at[back, :, pl.ds(start, stop - start)]
                copies.append((source, out.at[place]))
    for index, (source, target) in enumerate(copies):
        pltpu.make_async_copy(source, target, sem.at[index]).start()
    for index, (source, target) in enumerate(copies):
        pltpu.make_async_copy(source, target, sem.at[index]).wait()


def gather_rows(grid, shard, order, splits):
    rows, columns = shard.shape
    rounds = [shard] + [grid.shift(shard, OUTER, k) for k in range(1, grid.outer_size)]
    pieces = [((0, 0, 0, 0), jnp.stack(rounds))]
    for axis in order:
        more = []
        for amount in range(1, grid.sizes[axis]):
            for step, piece in pieces:
                moved = list(step)
                moved[axis] = amount
                more.append((tuple(moved), grid.shift(piece, axis, amount)))
        pieces = pieces + more
    outs = pl.pallas_call(
        functools.partial(place_kernel, grid, [step for step, _ in pieces], splits),
        out_shape=[
            jax.ShapeDtypeStruct((grid.owners, rows, stop - start), shard.dtype)
            for start, stop in splits
        ],
        in_specs=[pl.BlockSpec(memory_space=pl.ANY)] * len(pieces),
        out_specs=[pl.BlockSpec(memory_space=pl.ANY)] * len(splits),
        scratch_shapes=[pltpu.SemaphoreType.DMA((grid.owners * len(splits),))],
        cost_estimate=pl.CostEstimate(
            flops=0, transcendentals=0, bytes_accessed=4 * grid.owners * rows * columns
        ),
        name="place_rows",
    )(*[piece for _, piece in pieces])
    return [out.reshape(grid.owners * rows, out.shape[2]) for out in outs]


def scatter_rows(grid, total, order):
    columns = total.shape[1]
    rows = total.shape[0] // grid.owners
    digits = grid.digits()
    part = total.astype(jnp.bfloat16).reshape(grid.sizes + (rows, columns))
    for axis in tuple(order) + (OUTER,):
        size, digit = grid.sizes[axis], digits[axis]
        own = lax.dynamic_slice_in_dim(part, digit, 1, axis).astype(jnp.float32)
        for amount in range(1, size):
            sent = lax.dynamic_slice_in_dim(part, (digit + amount) % size, 1, axis)
            own = own + grid.shift(sent, axis, amount).astype(jnp.float32)
        part = own if axis == OUTER else own.astype(jnp.bfloat16)
    return part.reshape(rows, columns)


def head_of(array, head):
    lane = lax.broadcasted_iota(jnp.int32, array.shape, 1)
    inside = lane < HEAD_DIM if head == 0 else lane >= HEAD_DIM
    return jnp.where(inside, array, jnp.zeros_like(array))


def times_transposed(left, right):
    return lax.dot_general(
        left, right, (((1,), (1,)), ((), ())), preferred_element_type=jnp.float32
    )


def times(left, right):
    return lax.dot_general(
        left, right, (((1,), (0,)), ((), ())), preferred_element_type=jnp.float32
    )


def attend_kernel(q_ref, k_ref, v_ref, k_far_ref, v_far_ref, o_ref, log_ref):
    keys = (k_ref[...], k_far_ref[...])
    values = (v_ref[...].T, v_far_ref[...].T)
    query = q_ref[...]
    mixed, logs = [], []
    for head in range(2):
        rows = slice(head * HEAD_DIM, (head + 1) * HEAD_DIM)
        part = head_of(query, head)
        scores = [times_transposed(key, part) for key in keys]
        highest = functools.reduce(
            jnp.maximum, [jnp.max(score, axis=0, keepdims=True) for score in scores]
        )
        weights = [jnp.exp2((score - highest) * LOG2_SCALE) for score in scores]
        total = sum(jnp.sum(weight, axis=0, keepdims=True) for weight in weights)
        inverse = 1.0 / total
        probs = [(weight * inverse).astype(jnp.bfloat16) for weight in weights]
        mixed.append(sum(times(value[rows], prob) for value, prob in zip(values, probs)))
        logs.append(highest * LOG2_SCALE + jnp.log2(total))
    o_ref[...] = jnp.concatenate(mixed, axis=0).T.astype(o_ref.dtype)
    log_ref[0] = jnp.concatenate(logs, axis=0)


def attend_back_kernel(
    q_ref, k_ref, v_ref, k_far_ref, v_far_ref, log_ref, g_ref,
    dq_ref, d_ref, d_far_ref,
):
    width = q_ref.shape[1] * pl.num_programs(0)
    column = pl.multiple_of(pl.program_id(0) * 128, 128)
    second = pl.multiple_of(d_ref.shape[1] // 2 + pl.program_id(0) * 128, 128)
    keys = (k_ref[...], k_far_ref[...])
    keys_turned = [key.T for key in keys]
    values = (v_ref[...], v_far_ref[...])
    query, grad = q_ref[...], g_ref[...]
    scale = HEAD_DIM ** (-0.5)
    grad_query = []
    grad_keys, grad_values = [None, None], [None, None]
    for head in range(2):
        rows = slice(head * HEAD_DIM, (head + 1) * HEAD_DIM)
        part, grad_part = head_of(query, head), head_of(grad, head)
        log = log_ref[0, head : head + 1, :]
        probs = [
            jnp.exp2(times_transposed(key, part) * LOG2_SCALE - log) for key in keys
        ]
        pulls = [times_transposed(value, grad_part) for value in values]
        inner = sum(
            jnp.sum(prob * pull, axis=0, keepdims=True) for prob, pull in zip(probs, pulls)
        )
        scores = [
            (prob * (pull - inner)).astype(jnp.bfloat16) for prob, pull in zip(probs, pulls)
        ]
        grad_query.append(
            sum(times(key[rows], score) for key, score in zip(keys_turned, scores))
        )
        for side in range(2):
            more = times(scores[side], part)
            grad_keys[side] = more if head == 0 else grad_keys[side] + more
            more = times(probs[side].astype(jnp.bfloat16), grad_part)
            grad_values[side] = more if head == 0 else grad_values[side] + more
    dq_ref[...] = (jnp.concatenate(grad_query, axis=0).T * scale).astype(dq_ref.dtype)
    for side, out in enumerate((d_ref, d_far_ref)):
        out[:, pl.ds(column, 128)] = (grad_keys[side] * scale).astype(out.dtype)
        out[:, pl.ds(second, 128)] = grad_values[side].astype(out.dtype)


def block_specs(frames, far, blocks):
    return [
        pl.BlockSpec((frames, 128), lambda i: (0, i)),
        pl.BlockSpec((frames, 128), lambda i: (0, i)),
        pl.BlockSpec((frames, 128), lambda i: (0, i + blocks)),
        pl.BlockSpec((far, 128), lambda i: (0, i)),
        pl.BlockSpec((far, 128), lambda i: (0, i + blocks)),
    ]


def attend(query, pair, pair_far):
    frames, width = query.shape
    far, blocks = pair_far.shape[0], width // 128
    work = frames * (frames + far) * width
    return pl.pallas_call(
        attend_kernel,
        grid=(blocks,),
        in_specs=block_specs(frames, far, blocks),
        out_specs=[
            pl.BlockSpec((frames, 128), lambda i: (0, i)),
            pl.BlockSpec((1, 2, frames), lambda i: (i, 0, 0)),
        ],
        out_shape=[
            jax.ShapeDtypeStruct((frames, width), jnp.bfloat16),
            jax.ShapeDtypeStruct((blocks, 2, frames), jnp.float32),
        ],
        compiler_params=pltpu.CompilerParams(vmem_limit_bytes=VMEM_BYTES),
        cost_estimate=pl.CostEstimate(
            flops=16 * work, transcendentals=work // HEAD_DIM, bytes_accessed=8 * frames * width
        ),
        name="attend",
    )(query, pair, pair, pair_far, pair_far)


def attend_back(query, pair, pair_far, logs, grad):
    frames, width = query.shape
    far, blocks = pair_far.shape[0], width // 128
    work = frames * (frames + far) * width
    return pl.pallas_call(
        attend_back_kernel,
        grid=(blocks,),
        in_specs=block_specs(frames, far, blocks)
        + [
            pl.BlockSpec((1, 2, frames), lambda i: (i, 0, 0)),
            pl.BlockSpec((frames, 128), lambda i: (0, i)),
        ],
        out_specs=[
            pl.BlockSpec((frames, 128), lambda i: (0, i)),
            pl.BlockSpec((frames, 2 * width), lambda i: (0, 0)),
            pl.BlockSpec((far, 2 * width), lambda i: (0, 0)),
        ],
        out_shape=[
            jax.ShapeDtypeStruct((frames, width), jnp.bfloat16),
            jax.ShapeDtypeStruct((frames, 2 * width), jnp.bfloat16),
            jax.ShapeDtypeStruct((far, 2 * width), jnp.bfloat16),
        ],
        compiler_params=pltpu.CompilerParams(vmem_limit_bytes=VMEM_BYTES),
        cost_estimate=pl.CostEstimate(
            flops=40 * work, transcendentals=work // HEAD_DIM, bytes_accessed=16 * frames * width
        ),
        name="attend_back",
    )(query, pair, pair, pair_far, pair_far, logs, grad)


def normal_parts(rows):
    center = jnp.mean(rows, axis=-1, keepdims=True)
    spread = rows - center
    variance = jnp.mean(spread * spread, axis=-1, keepdims=True)
    rate = lax.rsqrt(variance + EPSILON)
    return spread * rate, rate


def normal_back(grad, rows, gain):
    unit, rate = normal_parts(rows)
    scaled = grad * gain
    pulled = rate * (
        scaled
        - jnp.mean(scaled, axis=-1, keepdims=True)
        - unit * jnp.mean(scaled * unit, axis=-1, keepdims=True)
    )
    return pulled, jnp.sum(grad * unit, axis=0), jnp.sum(grad, axis=0)


def gelu_exact(values):
    return jax.nn.gelu(values, approximate=False)


def outer_total(left, right):
    return lax.dot_general(
        left, right, (((0,), (0,)), ((), ())), preferred_element_type=jnp.float32
    )


def column_total(values):
    return jnp.sum(values.astype(jnp.float32), axis=0)


SMALL = (0, 1, 3, 5, 6, 7, 9, 11)


def gather_small(grid, params):
    shards = [params[slot].astype(jnp.bfloat16) for slot in SMALL]
    packed = jnp.concatenate([shard.reshape(1, -1) for shard in shards], axis=1)
    whole = lax.all_gather(packed, AXES, axis=0, tiled=True)
    found, offset = {}, 0
    for slot, shard in zip(SMALL, shards):
        amount = shard.size
        part = whole[:, offset : offset + amount].reshape((grid.owners,) + shard.shape)
        found[slot] = jnp.moveaxis(part, 0, 1).reshape(LAYERS, -1).astype(jnp.float32)
        offset += amount
    return found


def scatter_small(grid, totals):
    packed = jnp.concatenate(
        [
            jnp.moveaxis(total.reshape(LAYERS, grid.owners, -1), 1, 0).reshape(grid.owners, -1)
            for total in totals
        ],
        axis=1,
    )
    own = lax.psum_scatter(packed, AXES, scatter_dimension=0, tiled=True)
    pieces, offset = [], 0
    for total in totals:
        amount = total.size // grid.owners
        pieces.append(own[0, offset : offset + amount].reshape(LAYERS, -1))
        offset += amount
    return pieces


def layer_forward(grid, hidden, small, matrices):
    g1, s1, bm, bo, g2, s2, bu, bd = small
    w_query, w_pair, w_out, w_up, w_down = matrices
    width = hidden.shape[1]
    normed = (normal_parts(hidden)[0] * g1 + s1).astype(jnp.bfloat16)
    normed_far = jnp.concatenate(
        [grid.shift(normed, SEQ, amount) for amount in range(1, grid.seq_size)], axis=0
    )
    pair_bias = jnp.concatenate([jnp.zeros((width,), jnp.float32), bm[width:]])
    query = (times(normed, w_query) + bm[:width]).astype(jnp.bfloat16)
    pair = (times(normed, w_pair) + pair_bias).astype(jnp.bfloat16)
    pair_far = (times(normed_far, w_pair) + pair_bias).astype(jnp.bfloat16)
    attended, logs = attend(query, pair, pair_far)
    middle = hidden + (times(attended, w_out) + bo)
    normed_two = (normal_parts(middle)[0] * g2 + s2).astype(jnp.bfloat16)
    before = times(normed_two, w_up) + bu
    active = gelu_exact(before).astype(jnp.bfloat16)
    output = middle + (times(active, w_down) + bd)
    return output, (
        hidden, normed, normed_far, query, pair, pair_far, logs, attended, middle,
        normed_two, before, active,
    )


def layer_backward(grid, grad_hidden, kept, small, matrices):
    (
        hidden, normed, normed_far, query, pair, pair_far, logs, attended, middle,
        normed_two, before, active,
    ) = kept
    g1, s1, bm, bo, g2, s2, bu, bd = small
    w_query, w_pair, w_out, w_up, w_down = matrices
    frames, width = hidden.shape
    grad_down = grad_hidden.astype(jnp.bfloat16)
    down = scatter_rows(grid, outer_total(active, grad_down), (CORE, SEQ, CROSS))
    down_bias = column_total(grad_down)
    grad_active = times_transposed(grad_down, w_down)
    grad_before = jax.vjp(gelu_exact, before)[1](grad_active)[0].astype(jnp.bfloat16)
    up = scatter_rows(grid, outer_total(normed_two, grad_before), (CORE, CROSS, SEQ))
    up_bias = column_total(grad_before)
    grad_two = times_transposed(grad_before, w_up)
    pulled, gain_two, shift_two = normal_back(grad_two, middle, g2)
    grad_middle = grad_hidden + pulled
    grad_branch = grad_middle.astype(jnp.bfloat16)
    out = scatter_rows(grid, outer_total(attended, grad_branch), (CORE, SEQ, CROSS))
    out_bias = column_total(grad_branch)
    grad_attended = times_transposed(grad_branch, w_out).astype(jnp.bfloat16)
    grad_query, grad_pair, grad_far = attend_back(query, pair, pair_far, logs, grad_attended)
    far = times_transposed(grad_far, w_pair).astype(jnp.bfloat16)
    arrived = sum(
        grid.shift(
            far[(amount - 1) * frames : amount * frames], SEQ, grid.seq_size - amount
        ).astype(jnp.float32)
        for amount in range(1, grid.seq_size)
    )
    mixing = jnp.concatenate(
        [
            outer_total(normed, grad_query).astype(jnp.bfloat16),
            (outer_total(normed, grad_pair) + outer_total(normed_far, grad_far)).astype(
                jnp.bfloat16
            ),
        ],
        axis=1,
    )
    mixing = scatter_rows(grid, mixing, (CORE, CROSS, SEQ))
    mixing_bias = jnp.concatenate(
        [
            column_total(grad_query),
            column_total(grad_pair[:, width:]) + column_total(grad_far[:, width:]),
        ]
    )
    grad_normed = (
        times_transposed(grad_query, w_query) + times_transposed(grad_pair, w_pair) + arrived
    )
    pulled, gain_one, shift_one = normal_back(grad_normed, hidden, g1)
    return grad_middle + pulled, (
        gain_one, shift_one, mixing, mixing_bias, out, out_bias, gain_two, shift_two,
        up, up_bias, down, down_bias,
    )


def body(frames, cotangent, *params):
    grid = Grid()
    width = frames.shape[2]
    small = gather_small(grid, params)
    small = [[small[slot][layer] for slot in SMALL] for layer in range(LAYERS)]
    matrices = []
    for layer in range(LAYERS):
        mixing, out, up, down = [
            params[slot][layer].astype(jnp.bfloat16) for slot in (2, 4, 8, 10)
        ]
        first = gather_rows(
            grid,
            jnp.concatenate([mixing, out], axis=1),
            (CROSS, SEQ, CORE),
            ((0, width), (width, 3 * width), (3 * width, 4 * width)),
        )
        second = gather_rows(grid, up, (SEQ, CROSS, CORE), ((0, up.shape[1]),))
        third = gather_rows(grid, down, (CROSS, SEQ, CORE), ((0, width),))
        matrices.append(first + second + third)
    hidden = frames.reshape(-1, width)
    records = []
    for layer in range(LAYERS):
        hidden, kept = layer_forward(grid, hidden, small[layer], matrices[layer])
        records.append(kept)
    grad_hidden = cotangent.reshape(-1, width)
    shares = [None] * LAYERS
    for layer in reversed(range(LAYERS)):
        grad_hidden, shares[layer] = layer_backward(
            grid, grad_hidden, records[layer], small[layer], matrices[layer]
        )
    stacked = [jnp.stack([share[slot] for share in shares]) for slot in range(12)]
    for slot, piece in zip(SMALL, scatter_small(grid, [stacked[slot] for slot in SMALL])):
        stacked[slot] = piece
    return tuple([hidden.reshape(frames.shape), grad_hidden.reshape(frames.shape)] + stacked)


def solution(mesh):
    vector, matrix = P(None, AXES), P(None, AXES, None)
    whole = P("clip", "seq", None)
    params = tuple(matrix if slot in (2, 4, 8, 10) else vector for slot in range(12))
    return jax.shard_map(
        body,
        mesh=mesh,
        in_specs=(whole, whole) + params,
        out_specs=(whole, whole) + params,
        check_vma=False,
    )
```

```python
import functools
import math

import jax
import jax.numpy as jnp
from jax import lax
from jax.experimental import pallas as pl
from jax.experimental.pallas import tpu as pltpu
from jax.sharding import PartitionSpec as P

HEAD_DIM = 64
LAYERS = 2
EPSILON = 1e-05
AXES = ("clip", "seq")
LOG2_SCALE = HEAD_DIM ** (-0.5) * math.log2(math.e)
VMEM_BYTES = 56 * 1024 * 1024
QUICK = pl.CostEstimate(flops=1000, transcendentals=0, bytes_accessed=1000)


class Grid:
    def __init__(self):
        clips, self.seq_size = lax.axis_size("clip"), lax.axis_size("seq")
        self.outer_size = clips // 4
        self.owners = clips * self.seq_size
        self.sizes = (self.outer_size, 2, 2, self.seq_size)
        self.strides = (4 * self.seq_size, 2 * self.seq_size, self.seq_size, 1)

    def digits(self):
        clip, seq = lax.axis_index("clip"), lax.axis_index("seq")
        return (clip // 4, (clip // 2) % 2, clip % 2, seq)

    def shift(self, array, axis, amount):
        size, stride = self.sizes[axis], self.strides[axis]
        pairs = []
        for place in range(self.owners):
            digit = (place // stride) % size
            pairs.append((place, place + ((digit + amount) % size - digit) * stride))
        return lax.ppermute(array, AXES, pairs)


OUTER, CROSS, CORE, SEQ = 0, 1, 2, 3


class Traffic:
    def __init__(self):
        self.active = []

    def add(self, stages):
        found = {}
        self.active.append([stages, next(stages), found])
        return found

    def tick(self, *state):
        flying = [entry[1] for entry in self.active]
        state, flying = lax.optimization_barrier((list(state), flying))
        going = []
        for (stages, _, found), arrays in zip(self.active, flying):
            try:
                going.append([stages, stages.send(arrays), found])
            except StopIteration as end:
                found["value"] = end.value
        self.active = going
        return state[0] if len(state) == 1 else state


def around(grid, array, axis):
    return [grid.shift(array, axis, amount) for amount in range(1, grid.sizes[axis])]


def join(pieces):
    return jnp.concatenate(pieces, axis=0)


def spread(steps, axis, size):
    return [
        step[:axis] + (amount,) + step[axis + 1 :] for amount in range(size) for step in steps
    ]


def place_kernel(grid, steps, splits, *refs):
    count = len(steps)
    pieces, outs, sem = refs[:count], refs[count : count + len(splits)], refs[-1]
    digits = grid.digits()
    copies = []
    for piece, found in zip(pieces, steps):
        for index, step in enumerate(found):
            place = 0
            for axis in range(4):
                size = grid.sizes[axis]
                place = place * size + lax.rem(digits[axis] + size - step[axis], size)
            for out, (start, stop, blocks) in zip(outs, splits):
                size = (stop - start) // blocks
                for block in range(blocks):
                    source = piece.at[index, :, pl.ds(start + block * size, size)]
                    target = out.at[place * blocks + block]
                    copies.append(pltpu.make_async_copy(source, target, sem.at[len(copies)]))
    for copy in copies:
        copy.start()
    for copy in copies:
        copy.wait()


def gather_rows(grid, shard, splits):
    rows, columns = shard.shape
    own = shard[None]
    own, *rounds = yield [own] + around(grid, own, OUTER)
    half = max(grid.outer_size // 2, 1)
    line = [(back, 0, 0, 0) for back in range(grid.outer_size)]
    groups = [[own] + rounds[: half - 1], rounds[half - 1 :]]
    steps = [line[:half], line[half:]]
    orders = [(CROSS, SEQ), (SEQ, CROSS)]
    pieces = [join(group) for group in groups]
    for turn in range(2):
        moved = [around(grid, piece, order[turn]) for piece, order in zip(pieces, orders)]
        pieces, moved = yield pieces, moved
        if turn == 0:
            pieces = [join([piece] + more) for piece, more in zip(pieces, moved)]
            steps = [
                spread(step, order[turn], grid.sizes[order[turn]])
                for step, order in zip(steps, orders)
            ]
    steps = [
        spread(step, order[1], grid.sizes[order[1]]) for step, order in zip(steps, orders)
    ]
    steps = [
        part[start : start + piece.shape[0]]
        for part, piece in zip(steps, pieces)
        for start in range(0, len(part), piece.shape[0])
    ]
    pieces = [part for piece, more in zip(pieces, moved) for part in [piece] + more]
    far = [grid.shift(piece, CORE, 1) for piece in pieces]
    pieces, far = yield pieces, far
    steps = steps + [[step[:CORE] + (1,) + step[CORE + 1 :] for step in found] for found in steps]
    outs = pl.pallas_call(
        functools.partial(place_kernel, grid, steps, splits),
        out_shape=[
            jax.ShapeDtypeStruct(
                (grid.owners * blocks, rows, (stop - start) // blocks), shard.dtype
            )
            for start, stop, blocks in splits
        ],
        in_specs=[pl.BlockSpec(memory_space=pl.ANY)] * len(steps),
        out_specs=[pl.BlockSpec(memory_space=pltpu.VMEM)] * len(splits),
        scratch_shapes=[pltpu.SemaphoreType.DMA((grid.owners * sum(split[2] for split in splits),))],
        compiler_params=pltpu.CompilerParams(vmem_limit_bytes=VMEM_BYTES),
        cost_estimate=QUICK,
        name="place_rows",
    )(*pieces, *far)
    return [out.reshape(-1, out.shape[2]) for out in outs]


def exchange(grid, part, axis):
    size, digit = grid.sizes[axis], grid.digits()[axis]
    kept = lax.dynamic_slice_in_dim(part, digit, 1, axis)
    arrived = [
        grid.shift(lax.dynamic_slice_in_dim(part, (digit + amount) % size, 1, axis), axis, amount)
        for amount in range(1, size)
    ]
    return kept, arrived


def total_of(kept, arrived):
    return sum((piece.astype(jnp.float32) for piece in arrived), kept.astype(jnp.float32))


def by_core(grid, total):
    rows, columns = total.shape
    shape = grid.sizes + (rows // grid.owners, columns)
    core = grid.digits()[CORE]
    total = total.astype(jnp.bfloat16).reshape(shape)
    return [lax.dynamic_slice_in_dim(total, place, 1, CORE) for place in (core, 1 - core)]


def scatter_rows(grid, kept, sent):
    kept, arrived = yield kept, [grid.shift(sent, CORE, 1)]
    part = total_of(kept, arrived).astype(jnp.bfloat16)
    half = grid.outer_size // 2
    parts = [part[:half], part[half:]]
    orders = [(CROSS, SEQ), (SEQ, CROSS)]
    for turn in range(2):
        flying = yield [exchange(grid, part, order[turn]) for part, order in zip(parts, orders)]
        parts = [total_of(*entry).astype(jnp.bfloat16) for entry in flying]
    kept, arrived = yield exchange(grid, join(parts), OUTER)
    return total_of(kept, arrived).reshape(kept.shape[-2:])


def split_columns(rows_first, blocks):
    owners, rows, columns = rows_first.shape
    turned = rows_first.reshape(owners, blocks, rows // blocks, columns)
    return jnp.moveaxis(turned, 1, 2).reshape(owners * (rows // blocks), blocks * columns)


def turned_product(left, right):
    return lax.dot_general(
        left, right, (((0,), (0,)), ((), ())), preferred_element_type=jnp.float32
    )


def feed_shares_kernel(
    grid, normed_ref, before_ref, mixed_ref, branch_ref, active_ref, down_ref, kept_ref, sent_ref
):
    step = pl.program_id(0)
    first = lax.axis_index("clip") % 2 == 0
    outer, _, _, seq = grid.sizes
    width = normed_ref.shape[1]
    ups = pl.num_programs(0) - 1 - outer
    rows = width // grid.owners

    def store(total, low, column):
        for ref, here in ((kept_ref, True), (sent_ref, False)):
            part = jnp.where(first == here, total[:, :, 0], total[:, :, 1])
            part = part.reshape(-1, width).astype(ref.dtype)
            ref[pl.ds(low, part.shape[0]), pl.ds(column, width)] = part

    def by_owner(total):
        return total.reshape(outer, 2, 2, seq * rows, width)

    @pl.when(step < ups)
    def _():
        column = pl.multiple_of(step * width, 128)
        store(by_owner(turned_product(normed_ref[...], before_ref[...])), 0, column)

    @pl.when(step == ups)
    def _():
        total = turned_product(mixed_ref[...], branch_ref[...])
        store(by_owner(total), 0, pl.multiple_of(step * width, 128))

    @pl.when(step > ups)
    def _():
        total = turned_product(active_ref[...], down_ref[...])
        blocks = total.shape[0] // (4 * seq * rows)
        total = total.reshape(1, 2, 2, seq, blocks, rows, width)
        line = pl.multiple_of((step - ups - 1) * (2 * seq * rows), 2 * seq * rows)
        for block in range(blocks):
            store(
                total[:, :, :, :, block].reshape(1, 2, 2, seq * rows, width),
                line,
                pl.multiple_of((ups + 1 + block) * width, 128),
            )


def feed_shares(grid, normed, before, mixed, branch, active, down):
    frames, width = normed.shape
    units = before.shape[1]
    blocks, rows = units // width, width // grid.owners
    columns = 2 * units + width
    if rows % 8 or grid.outer_size != blocks:
        up = outer_total(normed, before)
        out = outer_total(mixed, branch)
        low = split_columns(outer_total(active, down).reshape(grid.owners, -1, width), blocks)
        return by_core(grid, jnp.concatenate([up, out, low], axis=1))
    whole = pl.BlockSpec((frames, width), lambda i: (0, 0))
    half = pl.BlockSpec((width // 2, columns), lambda i: (0, 0))
    pair = pl.pallas_call(
        functools.partial(feed_shares_kernel, grid),
        grid=(2 * blocks + 1,),
        in_specs=[
            whole,
            pl.BlockSpec((frames, width), lambda i: (0, jnp.minimum(i, blocks - 1))),
            whole,
            whole,
            pl.BlockSpec((frames, width), lambda i: (0, jnp.maximum(i - blocks - 1, 0))),
            whole,
        ],
        out_specs=[half, half],
        out_shape=[jax.ShapeDtypeStruct((width // 2, columns), jnp.bfloat16)] * 2,
        compiler_params=pltpu.CompilerParams(vmem_limit_bytes=VMEM_BYTES),
        cost_estimate=QUICK,
        name="feed_shares",
    )(normed, before, mixed, branch, active, down)
    shape = (grid.outer_size, 2, 1, grid.seq_size, rows, columns)
    return [part.reshape(shape) for part in pair]


def mixing_shares_kernel(grid, near_ref, far_ref, query_ref, pair_ref, pair_far_ref, *outs):
    step = pl.program_id(0)
    first = lax.axis_index("clip") % 2 == 0
    outer, _, _, seq = grid.sizes
    width = near_ref.shape[1]
    rows = width // grid.owners

    def store(total):
        total = total.reshape(outer, 2, 2, seq * rows, width)
        for ref, here in zip(outs, (True, False)):
            part = jnp.where(first == here, total[:, :, 0], total[:, :, 1])
            ref[...] = part.reshape(-1, width).astype(ref.dtype)

    @pl.when(step == 0)
    def _():
        store(turned_product(near_ref[...], query_ref[...]))

    @pl.when(step > 0)
    def _():
        store(
            turned_product(near_ref[...], pair_ref[...])
            + turned_product(far_ref[...], pair_far_ref[...])
        )


def mixing_shares(grid, near, far, query, pair, pair_far):
    frames, width = near.shape
    rows = width // grid.owners
    if rows % 8:
        total = jnp.concatenate(
            [
                outer_total(near, query),
                outer_total(near, pair) + outer_total(far, pair_far),
            ],
            axis=1,
        )
        return by_core(grid, total)
    near_spec = pl.BlockSpec((frames, width), lambda i: (0, 0))
    half = pl.BlockSpec((width // 2, width), lambda i: (0, i))
    parts = pl.pallas_call(
        functools.partial(mixing_shares_kernel, grid),
        grid=(3,),
        in_specs=[
            near_spec,
            pl.BlockSpec(far.shape, lambda i: (0, 0)),
            near_spec,
            pl.BlockSpec((frames, width), lambda i: (0, jnp.maximum(i - 1, 0))),
            pl.BlockSpec((far.shape[0], width), lambda i: (0, jnp.maximum(i - 1, 0))),
        ],
        out_specs=[half, half],
        out_shape=[jax.ShapeDtypeStruct((width // 2, 3 * width), jnp.bfloat16)] * 2,
        compiler_params=pltpu.CompilerParams(vmem_limit_bytes=VMEM_BYTES),
        cost_estimate=QUICK,
        name="mixing_shares",
    )(near, far, query, pair, pair_far)
    shape = (grid.outer_size, 2, 1, grid.seq_size, rows, 3 * width)
    return [part.reshape(shape) for part in parts]


def head_of(array, head):
    lane = lax.broadcasted_iota(jnp.int32, array.shape, 1)
    inside = lane < HEAD_DIM if head == 0 else lane >= HEAD_DIM
    return jnp.where(inside, array, jnp.zeros_like(array))


def times_transposed(left, right):
    return lax.dot_general(
        left, right, (((1,), (1,)), ((), ())), preferred_element_type=jnp.float32
    )


def times(left, right):
    return lax.dot_general(
        left, right, (((1,), (0,)), ((), ())), preferred_element_type=jnp.float32
    )


def attend_kernel(q_ref, k_ref, v_ref, k_far_ref, v_far_ref, o_ref, log_ref):
    keys = (k_ref[...], k_far_ref[...])
    values = (v_ref[...].T, v_far_ref[...].T)
    query = q_ref[...]
    mixed, logs = [], []
    for head in range(2):
        rows = slice(head * HEAD_DIM, (head + 1) * HEAD_DIM)
        part = head_of(query, head)
        scores = [times_transposed(key, part) for key in keys]
        highest = functools.reduce(
            jnp.maximum, [jnp.max(score, axis=0, keepdims=True) for score in scores]
        )
        weights = [jnp.exp2((score - highest) * LOG2_SCALE) for score in scores]
        total = sum(jnp.sum(weight, axis=0, keepdims=True) for weight in weights)
        inverse = 1.0 / total
        probs = [(weight * inverse).astype(jnp.bfloat16) for weight in weights]
        mixed.append(sum(times(value[rows], prob) for value, prob in zip(values, probs)))
        logs.append(highest * LOG2_SCALE + jnp.log2(total))
    o_ref[...] = jnp.concatenate(mixed, axis=0).T.astype(o_ref.dtype)
    log_ref[0] = jnp.concatenate(logs, axis=0)


def attend_back_kernel(
    q_ref, k_ref, v_ref, k_far_ref, v_far_ref, log_ref, g_ref,
    dq_ref, d_ref, d_far_ref,
):
    width = q_ref.shape[1] * pl.num_programs(0)
    column = pl.multiple_of(pl.program_id(0) * 128, 128)
    second = pl.multiple_of(d_ref.shape[1] // 2 + pl.program_id(0) * 128, 128)
    keys = (k_ref[...], k_far_ref[...])
    keys_turned = [key.T for key in keys]
    values = (v_ref[...], v_far_ref[...])
    query, grad = q_ref[...], g_ref[...]
    scale = HEAD_DIM ** (-0.5)
    grad_query = []
    grad_keys, grad_values = [None, None], [None, None]
    for head in range(2):
        rows = slice(head * HEAD_DIM, (head + 1) * HEAD_DIM)
        part, grad_part = head_of(query, head), head_of(grad, head)
        log = log_ref[0, head : head + 1, :]
        probs = [
            jnp.exp2(times_transposed(key, part) * LOG2_SCALE - log) for key in keys
        ]
        pulls = [times_transposed(value, grad_part) for value in values]
        inner = sum(
            jnp.sum(prob * pull, axis=0, keepdims=True) for prob, pull in zip(probs, pulls)
        )
        scores = [
            (prob * (pull - inner)).astype(jnp.bfloat16) for prob, pull in zip(probs, pulls)
        ]
        grad_query.append(
            sum(times(key[rows], score) for key, score in zip(keys_turned, scores))
        )
        for side in range(2):
            more = times(scores[side], part)
            grad_keys[side] = more if head == 0 else grad_keys[side] + more
            more = times(probs[side].astype(jnp.bfloat16), grad_part)
            grad_values[side] = more if head == 0 else grad_values[side] + more
    dq_ref[...] = (jnp.concatenate(grad_query, axis=0).T * scale).astype(dq_ref.dtype)
    for side, out in enumerate((d_ref, d_far_ref)):
        out[:, pl.ds(column, 128)] = (grad_keys[side] * scale).astype(out.dtype)
        out[:, pl.ds(second, 128)] = grad_values[side].astype(out.dtype)


def block_specs(frames, far, blocks):
    return [
        pl.BlockSpec((frames, 128), lambda i: (0, i)),
        pl.BlockSpec((frames, 128), lambda i: (0, i)),
        pl.BlockSpec((frames, 128), lambda i: (0, i + blocks)),
        pl.BlockSpec((far, 128), lambda i: (0, i)),
        pl.BlockSpec((far, 128), lambda i: (0, i + blocks)),
    ]


def attend(query, pair, pair_far):
    frames, width = query.shape
    far, blocks = pair_far.shape[0], width // 128
    return pl.pallas_call(
        attend_kernel,
        grid=(blocks,),
        in_specs=block_specs(frames, far, blocks),
        out_specs=[
            pl.BlockSpec((frames, 128), lambda i: (0, i)),
            pl.BlockSpec((1, 2, frames), lambda i: (i, 0, 0)),
        ],
        out_shape=[
            jax.ShapeDtypeStruct((frames, width), jnp.bfloat16),
            jax.ShapeDtypeStruct((blocks, 2, frames), jnp.float32),
        ],
        compiler_params=pltpu.CompilerParams(vmem_limit_bytes=VMEM_BYTES),
        cost_estimate=QUICK,
        name="attend",
    )(query, pair, pair, pair_far, pair_far)


def attend_back(query, pair, pair_far, logs, grad):
    frames, width = query.shape
    far, blocks = pair_far.shape[0], width // 128
    return pl.pallas_call(
        attend_back_kernel,
        grid=(blocks,),
        in_specs=block_specs(frames, far, blocks)
        + [
            pl.BlockSpec((1, 2, frames), lambda i: (i, 0, 0)),
            pl.BlockSpec((frames, 128), lambda i: (0, i)),
        ],
        out_specs=[
            pl.BlockSpec((frames, 128), lambda i: (0, i)),
            pl.BlockSpec((frames, 2 * width), lambda i: (0, 0)),
            pl.BlockSpec((far, 2 * width), lambda i: (0, 0)),
        ],
        out_shape=[
            jax.ShapeDtypeStruct((frames, width), jnp.bfloat16),
            jax.ShapeDtypeStruct((frames, 2 * width), jnp.bfloat16),
            jax.ShapeDtypeStruct((far, 2 * width), jnp.bfloat16),
        ],
        compiler_params=pltpu.CompilerParams(vmem_limit_bytes=VMEM_BYTES),
        cost_estimate=QUICK,
        name="attend_back",
    )(query, pair, pair, pair_far, pair_far, logs, grad)


def normal_parts(rows):
    center = jnp.mean(rows, axis=-1, keepdims=True)
    spread = rows - center
    variance = jnp.mean(spread * spread, axis=-1, keepdims=True)
    rate = lax.rsqrt(variance + EPSILON)
    return spread * rate, rate


def normal_back(grad, rows, gain):
    unit, rate = normal_parts(rows)
    scaled = grad * gain
    pulled = rate * (
        scaled
        - jnp.mean(scaled, axis=-1, keepdims=True)
        - unit * jnp.mean(scaled * unit, axis=-1, keepdims=True)
    )
    return pulled, jnp.sum(grad * unit, axis=0), jnp.sum(grad, axis=0)


def raise_kernel(left_ref, right_ref, bias_ref, active_ref, slope_ref):
    values = times(left_ref[...], right_ref[...]) + bias_ref[...]
    below = 0.5 + 0.5 * lax.erf(values * math.sqrt(0.5))
    density = jnp.exp(-0.5 * values * values) * (1.0 / math.sqrt(2.0 * math.pi))
    active_ref[...] = (values * below).astype(active_ref.dtype)
    slope_ref[...] = below + values * density


def raise_width(left, right, bias):
    frames, width = left.shape
    units = right.shape[1]
    tile = 512
    return pl.pallas_call(
        raise_kernel,
        grid=(units // tile,),
        in_specs=[
            pl.BlockSpec((frames, width), lambda i: (0, 0)),
            pl.BlockSpec((width, tile), lambda i: (0, i)),
            pl.BlockSpec((1, tile), lambda i: (0, i)),
        ],
        out_specs=[pl.BlockSpec((frames, tile), lambda i: (0, i))] * 2,
        out_shape=[
            jax.ShapeDtypeStruct((frames, units), jnp.bfloat16),
            jax.ShapeDtypeStruct((frames, units), jnp.float32),
        ],
        compiler_params=pltpu.CompilerParams(vmem_limit_bytes=VMEM_BYTES),
        cost_estimate=QUICK,
        name="raise_width",
    )(left, right, bias.reshape(1, -1))


def outer_total(left, right):
    return lax.dot_general(
        left, right, (((0,), (0,)), ((), ())), preferred_element_type=jnp.float32
    )


def column_total(values):
    return jnp.sum(values.astype(jnp.float32), axis=0)


SMALL = (0, 1, 3, 5, 6, 7, 9, 11)


def everywhere(grid, array):
    for axis in (OUTER, CROSS, SEQ, CORE):
        array = sum(around(grid, array, axis), array)
    return array


def gather_small(grid, params):
    place = lax.axis_index("clip") * grid.seq_size + lax.axis_index("seq")
    lanes = []
    for slot in SMALL:
        shard = params[slot].astype(jnp.bfloat16)
        empty = jnp.zeros((LAYERS, shard.shape[1] * grid.owners), jnp.bfloat16)
        lanes.append(lax.dynamic_update_slice_in_dim(empty, shard, place * shard.shape[1], 1))
    whole = everywhere(grid, jnp.concatenate(lanes, axis=1)).astype(jnp.float32)
    found, offset = [[] for _ in range(LAYERS)], 0
    for lane in lanes:
        for layer in range(LAYERS):
            found[layer].append(whole[layer, offset : offset + lane.shape[1]])
        offset += lane.shape[1]
    return found


def scatter_small(grid, totals):
    place = lax.axis_index("clip") * grid.seq_size + lax.axis_index("seq")
    whole = jnp.stack([jnp.concatenate(layer) for layer in totals])
    for axis in (CORE, SEQ, CROSS, OUTER):
        whole, moved = yield whole, around(grid, whole, axis)
        whole = sum(moved, whole)
    pieces, offset = [], 0
    for total in totals[0]:
        amount = total.shape[0] // grid.owners
        pieces.append(
            lax.dynamic_slice_in_dim(whole, offset + place * amount, amount, 1)
        )
        offset += total.shape[0]
    return pieces


def pair_of(normed, w_pair, bias):
    return (times(normed, w_pair) + bias).astype(jnp.bfloat16)


def body(frames, cotangent, *params):
    grid, traffic = Grid(), Traffic()
    width = frames.shape[2]
    rows = frames.shape[0] * frames.shape[1]
    units = params[8].shape[2]
    blocks = units // width
    shards = []
    for layer in range(LAYERS):
        mixing, out, up, down = [
            params[slot][layer].astype(jnp.bfloat16) for slot in (2, 4, 8, 10)
        ]
        shards.append((mixing, jnp.concatenate([out, up, split_columns(down[None], blocks)], 1)))
    edges = [width, 3 * width, 4 * width, 4 * width + units, 4 * width + 2 * units]
    starts = [0] + edges[:-1]
    splits = [(start, stop, 1) for start, stop in zip(starts, edges)]
    splits[-1] = splits[-1][:2] + (blocks,)
    behind = [(start - edges[1], stop - edges[1], count) for start, stop, count in splits[2:]]

    def normal(hidden, gain, shift):
        normed = (normal_parts(hidden)[0] * gain + shift).astype(jnp.bfloat16)
        return normed, join(around(grid, normed, SEQ))

    hidden = frames.reshape(rows, width)
    kept = [{} for _ in range(LAYERS)]

    first = shards[0][0]
    first, vectors = lax.optimization_barrier((first, [params[slot] for slot in SMALL]))
    mixing = traffic.add(gather_rows(grid, first, tuple(splits[:2])))
    small = gather_small(grid, dict(zip(SMALL, vectors)))
    hidden = traffic.tick(hidden)
    rest = traffic.add(gather_rows(grid, shards[0][1], tuple(behind)))
    normed, normed_far = normal(hidden, *small[0][:2])
    hidden, normed, normed_far = traffic.tick(hidden, normed, normed_far)
    hidden, normed, normed_far = traffic.tick(hidden, normed, normed_far)
    second = traffic.add(
        gather_rows(grid, jnp.concatenate(shards[1], axis=1), tuple(splits))
    )
    hidden, normed, normed_far = traffic.tick(hidden, normed, normed_far)
    for layer in range(LAYERS):
        g1, s1, bm, bo, g2, s2, bu, bd = small[layer]
        keep = kept[layer]
        if layer == 0:
            w_query, w_pair = mixing["value"]
        else:
            while "value" not in second:
                hidden, normed, normed_far = traffic.tick(hidden, normed, normed_far)
            w_query, w_pair, w_out, w_up, w_down = second["value"]
        query = (times(normed, w_query) + bm[:width]).astype(jnp.bfloat16)
        pair_bias = jnp.concatenate([jnp.zeros((width,), jnp.float32), bm[width:]])
        pair, pair_far = [pair_of(part, w_pair, pair_bias) for part in (normed, normed_far)]
        attended, logs = attend(query, pair, pair_far)
        keep.update(
            hidden=hidden, normed=normed, normed_far=normed_far, query=query, pair=pair,
            pair_far=pair_far, logs=logs, w_query=w_query, w_pair=w_pair,
        )
        if layer == 0:
            while "value" not in rest:
                attended = traffic.tick(attended)
            w_out, w_up, w_down = rest["value"]
        middle = hidden + (times(attended, w_out) + bo)
        normed_two = (normal_parts(middle)[0] * g2 + s2).astype(jnp.bfloat16)
        active, slope = raise_width(normed_two, w_up, bu)
        keep.update(
            attended=attended, middle=middle, normed_two=normed_two, active=active,
            slope=slope, w_out=w_out, w_up=w_up, w_down=w_down,
        )
        hidden = middle + (times(active, w_down) + bd)
        if layer + 1 < LAYERS:
            normed, normed_far = normal(hidden, *small[layer + 1][:2])

    grad_hidden = cotangent.reshape(rows, width)
    shares, totals = [None] * LAYERS, [None] * LAYERS
    for layer in reversed(range(LAYERS)):
        g1, s1, bm, bo, g2, s2, bu, bd = small[layer]
        keep = kept[layer]
        grad_down = grad_hidden.astype(jnp.bfloat16)
        grad_before = (times_transposed(grad_down, keep["w_down"]) * keep["slope"]).astype(
            jnp.bfloat16
        )
        down_bias = column_total(grad_down)
        grad_hidden, grad_down, grad_before = traffic.tick(grad_hidden, grad_down, grad_before)
        up_bias = column_total(grad_before)
        grad_two = times_transposed(grad_before, keep["w_up"])
        pulled, gain_two, shift_two = normal_back(grad_two, keep["middle"], g2)
        grad_middle = grad_hidden + pulled
        grad_branch = grad_middle.astype(jnp.bfloat16)
        out_bias = column_total(grad_branch)
        grad_attended = times_transposed(grad_branch, keep["w_out"]).astype(jnp.bfloat16)
        feed = feed_shares(
            grid, keep["normed_two"], grad_before, keep["attended"], grad_branch,
            keep["active"], grad_down,
        )
        feed, grad_middle, grad_attended = traffic.tick(feed, grad_middle, grad_attended)
        feed_share = traffic.add(scatter_rows(grid, *feed))
        grad_query, grad_pair, grad_far = attend_back(
            keep["query"], keep["pair"], keep["pair_far"], keep["logs"], grad_attended
        )
        grad_query, grad_pair, grad_far = traffic.tick(grad_query, grad_pair, grad_far)
        far = times_transposed(grad_far, keep["w_pair"]).astype(jnp.bfloat16)
        arrived = [
            grid.shift(far[(amount - 1) * rows : amount * rows], SEQ, grid.seq_size - amount)
            for amount in range(1, grid.seq_size)
        ]
        mixed = mixing_shares(
            grid, keep["normed"], keep["normed_far"], grad_query, grad_pair, grad_far
        )
        mixing_bias = jnp.concatenate(
            [
                column_total(grad_query),
                column_total(grad_pair[:, width:]) + column_total(grad_far[:, width:]),
            ]
        )
        grad_normed = times_transposed(grad_query, keep["w_query"]) + times_transposed(
            grad_pair, keep["w_pair"]
        )
        mixed, grad_normed, arrived = traffic.tick(mixed, grad_normed, arrived)
        mixed_share = traffic.add(scatter_rows(grid, *mixed))
        grad_normed = total_of(grad_normed, arrived)
        pulled, gain_one, shift_one = normal_back(grad_normed, keep["hidden"], g1)
        grad_hidden = grad_middle + pulled
        shares[layer] = (mixed_share, feed_share)
        totals[layer] = (
            gain_one, shift_one, mixing_bias, out_bias, gain_two, shift_two, up_bias, down_bias,
        )
    owned = traffic.add(scatter_small(grid, totals))
    while traffic.active:
        grad_hidden = traffic.tick(grad_hidden)
    stacked = dict(zip(SMALL, owned["value"]))
    stacked[2] = jnp.stack([layer[0]["value"] for layer in shares])
    feeds = [layer[1]["value"] for layer in shares]
    stacked[4] = jnp.stack([feed[:, units : units + width] for feed in feeds])
    stacked[8] = jnp.stack([feed[:, :units] for feed in feeds])
    lows = [feed[:, units + width :].reshape(-1, blocks, width) for feed in feeds]
    stacked[10] = jnp.stack([jnp.moveaxis(low, 1, 0).reshape(-1, width) for low in lows])
    return tuple(
        [hidden.reshape(frames.shape), grad_hidden.reshape(frames.shape)]
        + [stacked[slot] for slot in range(12)]
    )


def solution(mesh):
    vector, matrix = P(None, AXES), P(None, AXES, None)
    whole = P("clip", "seq", None)
    params = tuple(matrix if slot in (2, 4, 8, 10) else vector for slot in range(12))
    return jax.shard_map(
        body,
        mesh=mesh,
        in_specs=(whole, whole) + params,
        out_specs=(whole, whole) + params,
        check_vma=False,
    )
```

```python
import functools
import math

import jax
import jax.numpy as jnp
from jax import lax
from jax.experimental import pallas as pl
from jax.experimental.pallas import tpu as pltpu
from jax.sharding import PartitionSpec as P

HEAD_DIM = 64
LAYERS = 2
EPSILON = 1e-05
AXES = ("clip", "seq")
LOG2_SCALE = HEAD_DIM ** (-0.5) * math.log2(math.e)
VMEM_BYTES = 56 * 1024 * 1024
QUICK = pl.CostEstimate(flops=1000, transcendentals=0, bytes_accessed=1000)


class Grid:
    def __init__(self):
        clips, self.seq_size = lax.axis_size("clip"), lax.axis_size("seq")
        self.outer_size = clips // 4
        self.owners = clips * self.seq_size
        self.sizes = (self.outer_size, 2, 2, self.seq_size)
        self.strides = (4 * self.seq_size, 2 * self.seq_size, self.seq_size, 1)

    def digits(self):
        clip, seq = lax.axis_index("clip"), lax.axis_index("seq")
        return (clip // 4, (clip // 2) % 2, clip % 2, seq)

    def swap_outer(self, array, bit):
        flip = self.strides[OUTER] << bit
        return lax.ppermute(array, AXES, [(place, place ^ flip) for place in range(self.owners)])

    def outer_bits(self):
        return list(reversed(range(self.outer_size.bit_length() - 1)))

    def shift(self, array, axis, amount):
        size, stride = self.sizes[axis], self.strides[axis]
        pairs = []
        for place in range(self.owners):
            digit = (place // stride) % size
            pairs.append((place, place + ((digit + amount) % size - digit) * stride))
        return lax.ppermute(array, AXES, pairs)


OUTER, CROSS, CORE, SEQ = 0, 1, 2, 3


class Traffic:
    def __init__(self):
        self.active = []

    def add(self, stages):
        found = {}
        self.active.append([stages, next(stages), found])
        return found

    def tick(self, *state):
        flying = [entry[1] for entry in self.active]
        state, flying = lax.optimization_barrier((list(state), flying))
        going = []
        for (stages, _, found), arrays in zip(self.active, flying):
            try:
                going.append([stages, stages.send(arrays), found])
            except StopIteration as end:
                found["value"] = end.value
        self.active = going
        return state[0] if len(state) == 1 else state


def around(grid, array, axis):
    return [grid.shift(array, axis, amount) for amount in range(1, grid.sizes[axis])]


def join(pieces):
    return jnp.concatenate(pieces, axis=0)


def spread(steps, axis, size):
    return [
        step[:axis] + (amount,) + step[axis + 1 :] for amount in range(size) for step in steps
    ]


def place_kernel(grid, steps, splits, *refs):
    count = len(steps)
    pieces, outs, sem = refs[:count], refs[count : count + len(splits)], refs[-1]
    digits = grid.digits()
    copies = []
    for piece, found in zip(pieces, steps):
        for index, step in enumerate(found):
            place = 0
            for axis in range(4):
                size = grid.sizes[axis]
                place = place * size + lax.rem(digits[axis] + size - step[axis], size)
            for out, (start, stop, blocks) in zip(outs, splits):
                size = (stop - start) // blocks
                for block in range(blocks):
                    source = piece.at[index, :, pl.ds(start + block * size, size)]
                    target = out.at[place * blocks + block]
                    copies.append(pltpu.make_async_copy(source, target, sem.at[len(copies)]))
    for copy in copies:
        copy.start()
    for copy in copies:
        copy.wait()


def gather_rows(grid, shard, splits):
    rows, columns = shard.shape
    own = shard[None]
    own, *rounds = yield [own] + around(grid, own, OUTER)
    half = max(grid.outer_size // 2, 1)
    line = [(back, 0, 0, 0) for back in range(grid.outer_size)]
    groups = [[own] + rounds[: half - 1], rounds[half - 1 :]]
    steps = [line[:half], line[half:]]
    orders = [(CROSS, SEQ), (SEQ, CROSS)]
    pieces = [join(group) for group in groups]
    for turn in range(2):
        moved = [around(grid, piece, order[turn]) for piece, order in zip(pieces, orders)]
        pieces, moved = yield pieces, moved
        if turn == 0:
            pieces = [join([piece] + more) for piece, more in zip(pieces, moved)]
            steps = [
                spread(step, order[turn], grid.sizes[order[turn]])
                for step, order in zip(steps, orders)
            ]
    steps = [
        spread(step, order[1], grid.sizes[order[1]]) for step, order in zip(steps, orders)
    ]
    steps = [
        part[start : start + piece.shape[0]]
        for part, piece in zip(steps, pieces)
        for start in range(0, len(part), piece.shape[0])
    ]
    pieces = [part for piece, more in zip(pieces, moved) for part in [piece] + more]
    far = [grid.shift(piece, CORE, 1) for piece in pieces]
    steps = steps + [[step[:CORE] + (1,) + step[CORE + 1 :] for step in found] for found in steps]
    outs = pl.pallas_call(
        functools.partial(place_kernel, grid, steps, splits),
        out_shape=[
            jax.ShapeDtypeStruct(
                (grid.owners * blocks, rows, (stop - start) // blocks), shard.dtype
            )
            for start, stop, blocks in splits
        ],
        in_specs=[pl.BlockSpec(memory_space=pl.ANY)] * len(steps),
        out_specs=[pl.BlockSpec(memory_space=pltpu.VMEM)] * len(splits),
        scratch_shapes=[pltpu.SemaphoreType.DMA((grid.owners * sum(split[2] for split in splits),))],
        compiler_params=pltpu.CompilerParams(vmem_limit_bytes=VMEM_BYTES),
        cost_estimate=QUICK,
        name="place_rows",
    )(*pieces, *far)
    return [out.reshape(-1, out.shape[2]) for out in outs]


def exchange(grid, part, axis):
    size, digit = grid.sizes[axis], grid.digits()[axis]
    kept = lax.dynamic_slice_in_dim(part, digit, 1, axis)
    arrived = [
        grid.shift(lax.dynamic_slice_in_dim(part, (digit + amount) % size, 1, axis), axis, amount)
        for amount in range(1, size)
    ]
    return kept, arrived


def total_of(kept, arrived):
    return sum((piece.astype(jnp.float32) for piece in arrived), kept.astype(jnp.float32))


def by_core(grid, total):
    rows, columns = total.shape
    shape = grid.sizes + (rows // grid.owners, columns)
    core = grid.digits()[CORE]
    total = total.astype(jnp.bfloat16).reshape(shape)
    return [lax.dynamic_slice_in_dim(total, place, 1, CORE) for place in (core, 1 - core)]


def scatter_rows(grid, kept, sent):
    kept, arrived = yield kept, [grid.shift(sent, CORE, 1)]
    part = total_of(kept, arrived).astype(jnp.bfloat16)
    half = grid.outer_size // 2
    parts = [part[:half], part[half:]]
    orders = [(CROSS, SEQ), (SEQ, CROSS)]
    for turn in range(2):
        flying = yield [exchange(grid, part, order[turn]) for part, order in zip(parts, orders)]
        parts = [total_of(*entry).astype(jnp.bfloat16) for entry in flying]
    outer = grid.digits()[OUTER]
    for bit in grid.outer_bits():
        upper = ((outer >> bit) & 1) == 1
        low, high = parts
        kept, sent = jnp.where(upper, high, low), jnp.where(upper, low, high)
        kept, arrived = yield kept, [grid.swap_outer(sent, bit)]
        part = total_of(kept, arrived)
        if bit:
            part = part.astype(jnp.bfloat16)
            half = part.shape[0] // 2
            parts = [part[:half], part[half:]]
    return part.reshape(part.shape[-2:])


def split_columns(rows_first, blocks):
    owners, rows, columns = rows_first.shape
    turned = rows_first.reshape(owners, blocks, rows // blocks, columns)
    return jnp.moveaxis(turned, 1, 2).reshape(owners * (rows // blocks), blocks * columns)


def turned_product(left, right):
    return lax.dot_general(
        left, right, (((0,), (0,)), ((), ())), preferred_element_type=jnp.float32
    )


def store_shares(pair, total, low, columns):
    first = lax.axis_index("clip") % 2 == 0
    for ref, here in zip(pair, (True, False)):
        part = jnp.where(first == here, total[:, :, 0], total[:, :, 1])
        part = part.reshape(-1, part.shape[-1]).astype(ref.dtype)
        ref[pl.ds(low, part.shape[0]), columns] = part


def up_shares_kernel(grid, normed_ref, before_ref, mixed_ref, branch_ref, kept, sent, turned):
    step, ups = pl.program_id(0), pl.num_programs(0) - 1
    outer, _, _, seq = grid.sizes
    width = normed_ref.shape[1]
    shape = (outer, 2, 2, seq * width // grid.owners, width)

    @pl.when(step == 0)
    def _():
        turned[...] = normed_ref[...].T

    @pl.when(step < ups)
    def _():
        total = times(turned[...], before_ref[...]).reshape(shape)
        store_shares((kept, sent), total, 0, slice(None))

    @pl.when(step == ups)
    def _():
        total = turned_product(mixed_ref[...], branch_ref[...]).reshape(shape)
        store_shares((kept, sent), total, 0, slice(None))


def up_shares(grid, normed, before, mixed, branch):
    frames, width = normed.shape
    blocks, rows = before.shape[1] // width, width // grid.owners
    if rows % 8:
        total = [outer_total(normed, before), outer_total(mixed, branch)]
        return by_core(grid, jnp.concatenate(total, axis=1))
    columns = before.shape[1] + width
    whole = pl.BlockSpec((frames, width), lambda i: (0, 0))
    half = pl.BlockSpec((width // 2, width), lambda i: (0, i))
    parts = pl.pallas_call(
        functools.partial(up_shares_kernel, grid),
        grid=(blocks + 1,),
        in_specs=[
            whole,
            pl.BlockSpec((frames, width), lambda i: (0, jnp.minimum(i, blocks - 1))),
            whole,
            whole,
        ],
        out_specs=[half, half],
        out_shape=[jax.ShapeDtypeStruct((width // 2, columns), jnp.bfloat16)] * 2,
        scratch_shapes=[pltpu.VMEM((width, frames), jnp.bfloat16)],
        compiler_params=pltpu.CompilerParams(vmem_limit_bytes=VMEM_BYTES),
        cost_estimate=QUICK,
        name="up_shares",
    )(normed, before, mixed, branch)
    shape = (grid.outer_size, 2, 1, grid.seq_size, rows, columns)
    return [part.reshape(shape) for part in parts]


def both_shares_kernel(
    grid, normed_ref, before_ref, mixed_ref, branch_ref, near_ref, far_ref, query_ref, pair_ref,
    pair_far_ref, kept, sent, turned, turned_far,
):
    step, ups = pl.program_id(0), pl.num_programs(0) - 4
    outer, _, _, seq = grid.sizes
    width = normed_ref.shape[1]
    shape = (outer, 2, 2, seq * width // grid.owners, width)

    @pl.when(step == 0)
    def _():
        turned[...] = normed_ref[...].T

    @pl.when(step < ups)
    def _():
        total = times(turned[...], before_ref[...]).reshape(shape)
        store_shares((kept, sent), total, 0, slice(None))

    @pl.when(step == ups)
    def _():
        total = turned_product(mixed_ref[...], branch_ref[...]).reshape(shape)
        store_shares((kept, sent), total, 0, slice(None))

    @pl.when(step == ups + 1)
    def _():
        turned[...] = near_ref[...].T
        turned_far[...] = far_ref[...].T
        total = times(turned[...], query_ref[...]).reshape(shape)
        store_shares((kept, sent), total, 0, slice(None))

    @pl.when(step > ups + 1)
    def _():
        total = times(turned[...], pair_ref[...]) + times(turned_far[...], pair_far_ref[...])
        store_shares((kept, sent), total.reshape(shape), 0, slice(None))


def both_shares(grid, normed, before, mixed, branch, near, far, query, pair, pair_far):
    frames, width = normed.shape
    blocks, rows = before.shape[1] // width, width // grid.owners
    if rows % 8:
        pairs = zip(
            up_shares(grid, normed, before, mixed, branch),
            mixing_shares(grid, near, far, query, pair, pair_far),
        )
        return [jnp.concatenate(pair, axis=-1) for pair in pairs]
    columns = before.shape[1] + 4 * width
    whole = pl.BlockSpec((frames, width), lambda i: (0, 0))
    half = pl.BlockSpec((width // 2, width), lambda i: (0, i))

    def late(i):
        return (0, jnp.maximum(i - blocks - 2, 0))

    parts = pl.pallas_call(
        functools.partial(both_shares_kernel, grid),
        grid=(blocks + 4,),
        in_specs=[
            whole,
            pl.BlockSpec((frames, width), lambda i: (0, jnp.minimum(i, blocks - 1))),
            whole,
            whole,
            whole,
            pl.BlockSpec(far.shape, lambda i: (0, 0)),
            whole,
            pl.BlockSpec((frames, width), late),
            pl.BlockSpec((far.shape[0], width), late),
        ],
        out_specs=[half, half],
        out_shape=[jax.ShapeDtypeStruct((width // 2, columns), jnp.bfloat16)] * 2,
        scratch_shapes=[
            pltpu.VMEM((width, frames), jnp.bfloat16),
            pltpu.VMEM((width, far.shape[0]), jnp.bfloat16),
        ],
        compiler_params=pltpu.CompilerParams(vmem_limit_bytes=VMEM_BYTES),
        cost_estimate=QUICK,
        name="both_shares",
    )(normed, before, mixed, branch, near, far, query, pair, pair_far)
    shape = (grid.outer_size, 2, 1, grid.seq_size, rows, columns)
    return [part.reshape(shape) for part in parts]


def low_shares_kernel(grid, rows, active_ref, down_ref, kept, sent):
    seq = grid.seq_size
    width = down_ref.shape[1]
    total = turned_product(active_ref[...], down_ref[...])
    blocks = total.shape[0] // (4 * seq * rows)
    total = total.reshape(1, 2, 2, seq, blocks, rows, width)
    for block in range(blocks):
        part = total[:, :, :, :, block].reshape(1, 2, 2, seq * rows, width)
        store_shares((kept, sent), part, 0, slice(block * width, (block + 1) * width))


def low_shares(grid, active, down):
    frames, width = down.shape
    units = active.shape[1]
    blocks, rows = units // width, width // grid.owners
    if rows % 8:
        total = outer_total(active, down).reshape(grid.owners, -1, width)
        return by_core(grid, split_columns(total, blocks))
    line = units // grid.outer_size
    half = pl.BlockSpec((width // (2 * grid.outer_size), units), lambda i: (i, 0))
    parts = pl.pallas_call(
        functools.partial(low_shares_kernel, grid, rows),
        grid=(grid.outer_size,),
        in_specs=[
            pl.BlockSpec((frames, line), lambda i: (0, i)),
            pl.BlockSpec((frames, width), lambda i: (0, 0)),
        ],
        out_specs=[half, half],
        out_shape=[jax.ShapeDtypeStruct((width // 2, units), jnp.bfloat16)] * 2,
        compiler_params=pltpu.CompilerParams(vmem_limit_bytes=VMEM_BYTES),
        cost_estimate=QUICK,
        name="low_shares",
    )(active, down)
    shape = (grid.outer_size, 2, 1, grid.seq_size, rows, units)
    return [part.reshape(shape) for part in parts]


def mixing_shares_kernel(
    grid, near_ref, far_ref, query_ref, pair_ref, pair_far_ref, kept, sent, turned, turned_far
):
    step = pl.program_id(0)
    outer, _, _, seq = grid.sizes
    width = near_ref.shape[1]
    shape = (outer, 2, 2, seq * width // grid.owners, width)

    @pl.when(step == 0)
    def _():
        turned[...] = near_ref[...].T
        turned_far[...] = far_ref[...].T
        total = times(turned[...], query_ref[...]).reshape(shape)
        store_shares((kept, sent), total, 0, slice(None))

    @pl.when(step > 0)
    def _():
        total = times(turned[...], pair_ref[...]) + times(turned_far[...], pair_far_ref[...])
        store_shares((kept, sent), total.reshape(shape), 0, slice(None))


def mixing_shares(grid, near, far, query, pair, pair_far):
    frames, width = near.shape
    rows = width // grid.owners
    if rows % 8:
        total = jnp.concatenate(
            [
                outer_total(near, query),
                outer_total(near, pair) + outer_total(far, pair_far),
            ],
            axis=1,
        )
        return by_core(grid, total)
    near_spec = pl.BlockSpec((frames, width), lambda i: (0, 0))
    half = pl.BlockSpec((width // 2, width), lambda i: (0, i))
    parts = pl.pallas_call(
        functools.partial(mixing_shares_kernel, grid),
        grid=(3,),
        in_specs=[
            near_spec,
            pl.BlockSpec(far.shape, lambda i: (0, 0)),
            near_spec,
            pl.BlockSpec((frames, width), lambda i: (0, jnp.maximum(i - 1, 0))),
            pl.BlockSpec((far.shape[0], width), lambda i: (0, jnp.maximum(i - 1, 0))),
        ],
        out_specs=[half, half],
        out_shape=[jax.ShapeDtypeStruct((width // 2, 3 * width), jnp.bfloat16)] * 2,
        scratch_shapes=[
            pltpu.VMEM((width, frames), jnp.bfloat16),
            pltpu.VMEM((width, far.shape[0]), jnp.bfloat16),
        ],
        compiler_params=pltpu.CompilerParams(vmem_limit_bytes=VMEM_BYTES),
        cost_estimate=QUICK,
        name="mixing_shares",
    )(near, far, query, pair, pair_far)
    shape = (grid.outer_size, 2, 1, grid.seq_size, rows, 3 * width)
    return [part.reshape(shape) for part in parts]


def head_of(array, head):
    lane = lax.broadcasted_iota(jnp.int32, array.shape, 1)
    inside = lane < HEAD_DIM if head == 0 else lane >= HEAD_DIM
    return jnp.where(inside, array, jnp.zeros_like(array))


def times_transposed(left, right):
    return lax.dot_general(
        left, right, (((1,), (1,)), ((), ())), preferred_element_type=jnp.float32
    )


def times(left, right):
    return lax.dot_general(
        left, right, (((1,), (0,)), ((), ())), preferred_element_type=jnp.float32
    )


def attend_kernel(q_ref, k_ref, v_ref, k_far_ref, v_far_ref, o_ref, log_ref):
    keys = (k_ref[...], k_far_ref[...])
    values = (v_ref[...].T, v_far_ref[...].T)
    query = q_ref[...]
    mixed, logs = [], []
    for head in range(2):
        rows = slice(head * HEAD_DIM, (head + 1) * HEAD_DIM)
        part = head_of(query, head)
        scores = [times_transposed(key, part) for key in keys]
        highest = functools.reduce(
            jnp.maximum, [jnp.max(score, axis=0, keepdims=True) for score in scores]
        )
        weights = [jnp.exp2((score - highest) * LOG2_SCALE) for score in scores]
        total = sum(jnp.sum(weight, axis=0, keepdims=True) for weight in weights)
        inverse = 1.0 / total
        probs = [(weight * inverse).astype(jnp.bfloat16) for weight in weights]
        mixed.append(sum(times(value[rows], prob) for value, prob in zip(values, probs)))
        logs.append(highest * LOG2_SCALE + jnp.log2(total))
    o_ref[...] = jnp.concatenate(mixed, axis=0).T.astype(o_ref.dtype)
    log_ref[0] = jnp.concatenate(logs, axis=0)


def attend_back_kernel(
    q_ref, k_ref, v_ref, k_far_ref, v_far_ref, log_ref, g_ref,
    dq_ref, d_ref, d_far_ref,
):
    width = q_ref.shape[1] * pl.num_programs(0)
    column = pl.multiple_of(pl.program_id(0) * 128, 128)
    second = pl.multiple_of(d_ref.shape[1] // 2 + pl.program_id(0) * 128, 128)
    keys = (k_ref[...], k_far_ref[...])
    keys_turned = [key.T for key in keys]
    values = (v_ref[...], v_far_ref[...])
    query, grad = q_ref[...], g_ref[...]
    scale = HEAD_DIM ** (-0.5)
    grad_query = []
    grad_keys, grad_values = [None, None], [None, None]
    for head in range(2):
        rows = slice(head * HEAD_DIM, (head + 1) * HEAD_DIM)
        part, grad_part = head_of(query, head), head_of(grad, head)
        log = log_ref[0, head : head + 1, :]
        probs = [
            jnp.exp2(times_transposed(key, part) * LOG2_SCALE - log) for key in keys
        ]
        pulls = [times_transposed(value, grad_part) for value in values]
        inner = sum(
            jnp.sum(prob * pull, axis=0, keepdims=True) for prob, pull in zip(probs, pulls)
        )
        scores = [
            (prob * (pull - inner)).astype(jnp.bfloat16) for prob, pull in zip(probs, pulls)
        ]
        grad_query.append(
            sum(times(key[rows], score) for key, score in zip(keys_turned, scores))
        )
        for side in range(2):
            more = times(scores[side], part)
            grad_keys[side] = more if head == 0 else grad_keys[side] + more
            more = times(probs[side].astype(jnp.bfloat16), grad_part)
            grad_values[side] = more if head == 0 else grad_values[side] + more
    dq_ref[...] = (jnp.concatenate(grad_query, axis=0).T * scale).astype(dq_ref.dtype)
    for side, out in enumerate((d_ref, d_far_ref)):
        out[:, pl.ds(column, 128)] = (grad_keys[side] * scale).astype(out.dtype)
        out[:, pl.ds(second, 128)] = grad_values[side].astype(out.dtype)


def block_specs(frames, far, blocks):
    return [
        pl.BlockSpec((frames, 128), lambda i: (0, i)),
        pl.BlockSpec((frames, 128), lambda i: (0, i)),
        pl.BlockSpec((frames, 128), lambda i: (0, i + blocks)),
        pl.BlockSpec((far, 128), lambda i: (0, i)),
        pl.BlockSpec((far, 128), lambda i: (0, i + blocks)),
    ]


def attend(query, pair, pair_far):
    frames, width = query.shape
    far, blocks = pair_far.shape[0], width // 128
    return pl.pallas_call(
        attend_kernel,
        grid=(blocks,),
        in_specs=block_specs(frames, far, blocks),
        out_specs=[
            pl.BlockSpec((frames, 128), lambda i: (0, i)),
            pl.BlockSpec((1, 2, frames), lambda i: (i, 0, 0)),
        ],
        out_shape=[
            jax.ShapeDtypeStruct((frames, width), jnp.bfloat16),
            jax.ShapeDtypeStruct((blocks, 2, frames), jnp.float32),
        ],
        compiler_params=pltpu.CompilerParams(vmem_limit_bytes=VMEM_BYTES),
        cost_estimate=QUICK,
        name="attend",
    )(query, pair, pair, pair_far, pair_far)


def attend_back(query, pair, pair_far, logs, grad):
    frames, width = query.shape
    far, blocks = pair_far.shape[0], width // 128
    return pl.pallas_call(
        attend_back_kernel,
        grid=(blocks,),
        in_specs=block_specs(frames, far, blocks)
        + [
            pl.BlockSpec((1, 2, frames), lambda i: (i, 0, 0)),
            pl.BlockSpec((frames, 128), lambda i: (0, i)),
        ],
        out_specs=[
            pl.BlockSpec((frames, 128), lambda i: (0, i)),
            pl.BlockSpec((frames, 2 * width), lambda i: (0, 0)),
            pl.BlockSpec((far, 2 * width), lambda i: (0, 0)),
        ],
        out_shape=[
            jax.ShapeDtypeStruct((frames, width), jnp.bfloat16),
            jax.ShapeDtypeStruct((frames, 2 * width), jnp.bfloat16),
            jax.ShapeDtypeStruct((far, 2 * width), jnp.bfloat16),
        ],
        compiler_params=pltpu.CompilerParams(vmem_limit_bytes=VMEM_BYTES),
        cost_estimate=QUICK,
        name="attend_back",
    )(query, pair, pair, pair_far, pair_far, logs, grad)


def normal_parts(rows):
    center = jnp.mean(rows, axis=-1, keepdims=True)
    spread = rows - center
    variance = jnp.mean(spread * spread, axis=-1, keepdims=True)
    rate = lax.rsqrt(variance + EPSILON)
    return spread * rate, rate


def normal_back(grad, rows, gain):
    unit, rate = normal_parts(rows)
    scaled = grad * gain
    pulled = rate * (
        scaled
        - jnp.mean(scaled, axis=-1, keepdims=True)
        - unit * jnp.mean(scaled * unit, axis=-1, keepdims=True)
    )
    return pulled, jnp.sum(grad * unit, axis=0), jnp.sum(grad, axis=0)


def raise_kernel(left_ref, right_ref, bias_ref, active_ref, slope_ref):
    values = times(left_ref[...], right_ref[...]) + bias_ref[...]
    below = 0.5 + 0.5 * lax.erf(values * math.sqrt(0.5))
    density = jnp.exp(-0.5 * values * values) * (1.0 / math.sqrt(2.0 * math.pi))
    active_ref[...] = (values * below).astype(active_ref.dtype)
    slope_ref[...] = below + values * density


def raise_width(left, right, bias):
    frames, width = left.shape
    units = right.shape[1]
    tile = 512
    return pl.pallas_call(
        raise_kernel,
        grid=(units // tile,),
        in_specs=[
            pl.BlockSpec((frames, width), lambda i: (0, 0)),
            pl.BlockSpec((width, tile), lambda i: (0, i)),
            pl.BlockSpec((1, tile), lambda i: (0, i)),
        ],
        out_specs=[pl.BlockSpec((frames, tile), lambda i: (0, i))] * 2,
        out_shape=[
            jax.ShapeDtypeStruct((frames, units), jnp.bfloat16),
            jax.ShapeDtypeStruct((frames, units), jnp.float32),
        ],
        compiler_params=pltpu.CompilerParams(vmem_limit_bytes=VMEM_BYTES),
        cost_estimate=QUICK,
        name="raise_width",
    )(left, right, bias.reshape(1, -1))


def outer_total(left, right):
    return lax.dot_general(
        left, right, (((0,), (0,)), ((), ())), preferred_element_type=jnp.float32
    )


def column_total(values):
    return jnp.sum(values.astype(jnp.float32), axis=0)


SMALL = (0, 1, 3, 5, 6, 7, 9, 11)


def everywhere(grid, array):
    for axis in (OUTER, CROSS, SEQ, CORE):
        array = sum(around(grid, array, axis), array)
    return array


def gather_small(grid, params):
    place = lax.axis_index("clip") * grid.seq_size + lax.axis_index("seq")
    lanes = []
    for slot in SMALL:
        shard = params[slot].astype(jnp.bfloat16)
        empty = jnp.zeros((LAYERS, shard.shape[1] * grid.owners), jnp.bfloat16)
        lanes.append(lax.dynamic_update_slice_in_dim(empty, shard, place * shard.shape[1], 1))
    whole = everywhere(grid, jnp.concatenate(lanes, axis=1)).astype(jnp.float32)
    found, offset = [[] for _ in range(LAYERS)], 0
    for lane in lanes:
        for layer in range(LAYERS):
            found[layer].append(whole[layer, offset : offset + lane.shape[1]])
        offset += lane.shape[1]
    return found


def scatter_small(grid, totals):
    place = lax.axis_index("clip") * grid.seq_size + lax.axis_index("seq")
    lengths = [total.shape[0] for total in totals[0]]
    starts = [sum(lengths[:index]) for index in range(len(lengths) + 1)]
    whole = sum(
        jnp.pad(
            total[None],
            ((layer, LAYERS - 1 - layer), (starts[index], starts[-1] - starts[index + 1])),
        )
        for layer in range(LAYERS)
        for index, total in enumerate(totals[layer])
    )
    for axis in (CORE, SEQ, CROSS):
        whole, moved = yield whole, around(grid, whole, axis)
        whole = sum(moved, whole)
    for bit in grid.outer_bits():
        whole, moved = yield whole, grid.swap_outer(whole, bit)
        whole = whole + moved
    pieces, offset = [], 0
    for total in totals[0]:
        amount = total.shape[0] // grid.owners
        pieces.append(
            lax.dynamic_slice_in_dim(whole, offset + place * amount, amount, 1)
        )
        offset += total.shape[0]
    return pieces


def pair_of(normed, w_pair, bias):
    return (times(normed, w_pair) + bias).astype(jnp.bfloat16)


def body(frames, cotangent, *params):
    grid, traffic = Grid(), Traffic()
    width = frames.shape[2]
    rows = frames.shape[0] * frames.shape[1]
    units = params[8].shape[2]
    blocks = units // width
    shards = []
    for layer in range(LAYERS):
        mixing, out, up, down = [
            params[slot][layer].astype(jnp.bfloat16) for slot in (2, 4, 8, 10)
        ]
        shards.append((mixing, jnp.concatenate([out, up, split_columns(down[None], blocks)], 1)))
    edges = [width, 3 * width, 4 * width, 4 * width + units, 4 * width + 2 * units]
    starts = [0] + edges[:-1]
    splits = [(start, stop, 1) for start, stop in zip(starts, edges)]
    splits[-1] = splits[-1][:2] + (blocks,)
    behind = [(start - edges[1], stop - edges[1], count) for start, stop, count in splits[2:]]

    def normal(hidden, gain, shift):
        normed = (normal_parts(hidden)[0] * gain + shift).astype(jnp.bfloat16)
        return normed, join(around(grid, normed, SEQ))

    hidden = frames.reshape(rows, width)
    kept = [{} for _ in range(LAYERS)]

    first = shards[0][0]
    first, vectors = lax.optimization_barrier((first, [params[slot] for slot in SMALL]))
    mixing = traffic.add(gather_rows(grid, first, tuple(splits[:2])))
    small = gather_small(grid, dict(zip(SMALL, vectors)))
    hidden = traffic.tick(hidden)
    rest = traffic.add(gather_rows(grid, shards[0][1], tuple(behind)))
    normed, normed_far = normal(hidden, *small[0][:2])
    last = [jnp.concatenate([shards[1][0], shards[1][1][:, : width + units]], axis=1),
            params[10][1].astype(jnp.bfloat16)]
    hidden, normed, normed_far, last = traffic.tick(hidden, normed, normed_far, last)
    wide, w_last = [lax.all_gather(part, AXES, axis=0, tiled=True) for part in last]
    second = {"value": [wide[:, start:stop] for start, stop, _ in splits[:-1]] + [w_last]}
    hidden, normed, normed_far = traffic.tick(hidden, normed, normed_far)
    for layer in range(LAYERS):
        g1, s1, bm, bo, g2, s2, bu, bd = small[layer]
        keep = kept[layer]
        if layer == 0:
            while "value" not in mixing:
                hidden, normed, normed_far = traffic.tick(hidden, normed, normed_far)
            w_query, w_pair = mixing["value"]
        else:
            while "value" not in second:
                hidden, normed, normed_far = traffic.tick(hidden, normed, normed_far)
            w_query, w_pair, w_out, w_up, w_down = second["value"]
        query = (times(normed, w_query) + bm[:width]).astype(jnp.bfloat16)
        pair_bias = jnp.concatenate([jnp.zeros((width,), jnp.float32), bm[width:]])
        pair, pair_far = [pair_of(part, w_pair, pair_bias) for part in (normed, normed_far)]
        attended, logs = attend(query, pair, pair_far)
        keep.update(
            hidden=hidden, normed=normed, normed_far=normed_far, query=query, pair=pair,
            pair_far=pair_far, logs=logs, w_query=w_query, w_pair=w_pair,
        )
        if layer == 0:
            while "value" not in rest:
                attended = traffic.tick(attended)
            w_out, w_up, w_down = rest["value"]
        middle = hidden + (times(attended, w_out) + bo)
        normed_two = (normal_parts(middle)[0] * g2 + s2).astype(jnp.bfloat16)
        active, slope = raise_width(normed_two, w_up, bu)
        keep.update(
            attended=attended, middle=middle, normed_two=normed_two, active=active,
            slope=slope, w_out=w_out, w_up=w_up, w_down=w_down,
        )
        hidden = middle + (times(active, w_down) + bd)
        if layer + 1 < LAYERS:
            normed, normed_far = normal(hidden, *small[layer + 1][:2])

    grad_hidden = cotangent.reshape(rows, width)
    shares, totals = [None] * LAYERS, [None] * LAYERS
    for layer in reversed(range(LAYERS)):
        g1, s1, bm, bo, g2, s2, bu, bd = small[layer]
        keep = kept[layer]
        grad_down = grad_hidden.astype(jnp.bfloat16)
        grad_before = (times_transposed(grad_down, keep["w_down"]) * keep["slope"]).astype(
            jnp.bfloat16
        )
        down_bias = column_total(grad_down)
        low = low_shares(grid, keep["active"], grad_down)
        if layer + 1 < LAYERS:
            low, grad_hidden, grad_before = traffic.tick(low, grad_hidden, grad_before)
            low_share = traffic.add(scatter_rows(grid, *low))
        up_bias = column_total(grad_before)
        grad_two = times_transposed(grad_before, keep["w_up"])
        pulled, gain_two, shift_two = normal_back(grad_two, keep["middle"], g2)
        grad_middle = grad_hidden + pulled
        grad_branch = grad_middle.astype(jnp.bfloat16)
        out_bias = column_total(grad_branch)
        grad_attended = times_transposed(grad_branch, keep["w_out"]).astype(jnp.bfloat16)
        operands = (keep["normed_two"], grad_before, keep["attended"], grad_branch)
        if layer + 1 < LAYERS:
            up = up_shares(grid, *operands)
            up, grad_middle, grad_attended = traffic.tick(up, grad_middle, grad_attended)
            up_share = traffic.add(scatter_rows(grid, *up))
        else:
            low, grad_middle, grad_attended = traffic.tick(low, grad_middle, grad_attended)
            low_share = traffic.add(scatter_rows(grid, *low))
        grad_query, grad_pair, grad_far = attend_back(
            keep["query"], keep["pair"], keep["pair_far"], keep["logs"], grad_attended
        )
        grad_query, grad_pair, grad_far, operands = traffic.tick(
            grad_query, grad_pair, grad_far, operands
        )
        far = times_transposed(grad_far, keep["w_pair"]).astype(jnp.bfloat16)
        arrived = [
            grid.shift(far[(amount - 1) * rows : amount * rows], SEQ, grid.seq_size - amount)
            for amount in range(1, grid.seq_size)
        ]
        far, grad_query, grad_pair, grad_far, operands = lax.optimization_barrier(
            (far, grad_query, grad_pair, grad_far, operands)
        )
        attention = (keep["normed"], keep["normed_far"], grad_query, grad_pair, grad_far)
        if layer + 1 == LAYERS:
            mixed = both_shares(grid, *operands, *attention)
        else:
            mixed = mixing_shares(grid, *attention)
        mixing_bias = jnp.concatenate(
            [
                column_total(grad_query),
                column_total(grad_pair[:, width:]) + column_total(grad_far[:, width:]),
            ]
        )
        grad_normed = times_transposed(grad_query, keep["w_query"]) + times_transposed(
            grad_pair, keep["w_pair"]
        )
        grad_normed = total_of(grad_normed, arrived)
        pulled, gain_one, shift_one = normal_back(grad_normed, keep["hidden"], g1)
        grad_hidden = grad_middle + pulled
        mixed, grad_hidden = traffic.tick(mixed, grad_hidden)
        mixed_share = traffic.add(scatter_rows(grid, *mixed))
        if layer + 1 == LAYERS:
            up_share = mixed_share
        shares[layer] = (mixed_share, up_share, low_share)
        totals[layer] = (
            gain_one, shift_one, mixing_bias, out_bias, gain_two, shift_two, up_bias, down_bias,
        )
    owned = traffic.add(scatter_small(grid, totals))
    while traffic.active:
        grad_hidden = traffic.tick(grad_hidden)
    stacked = dict(zip(SMALL, owned["value"]))
    values = [[share["value"] for share in layer] for layer in shares]
    stacked[2] = jnp.stack([value[0][:, -3 * width :] for value in values])
    stacked[4] = jnp.stack([value[1][:, units : units + width] for value in values])
    stacked[8] = jnp.stack([value[1][:, :units] for value in values])
    lows = [value[2].reshape(-1, blocks, width) for value in values]
    stacked[10] = jnp.stack([jnp.moveaxis(low, 1, 0).reshape(-1, width) for low in lows])
    return tuple(
        [hidden.reshape(frames.shape), grad_hidden.reshape(frames.shape)]
        + [stacked[slot] for slot in range(12)]
    )


def solution(mesh):
    vector, matrix = P(None, AXES), P(None, AXES, None)
    whole = P("clip", "seq", None)
    params = tuple(matrix if slot in (2, 4, 8, 10) else vector for slot in range(12))
    return jax.shard_map(
        body,
        mesh=mesh,
        in_specs=(whole, whole) + params,
        out_specs=(whole, whole) + params,
        check_vma=False,
    )
```

```python
import functools
import math

import jax
import jax.numpy as jnp
from jax import lax
from jax.experimental import pallas as pl
from jax.experimental.pallas import tpu as pltpu
from jax.sharding import PartitionSpec as P

HEAD_DIM = 64
LAYERS = 2
EPSILON = 1e-05
AXES = ("clip", "seq")
LOG2_SCALE = HEAD_DIM ** (-0.5) * math.log2(math.e)
VMEM_BYTES = 56 * 1024 * 1024
QUICK = pl.CostEstimate(flops=1000, transcendentals=0, bytes_accessed=1000)


class Grid:
    def __init__(self):
        clips, self.seq_size = lax.axis_size("clip"), lax.axis_size("seq")
        self.outer_size = clips // 4
        self.owners = clips * self.seq_size
        self.sizes = (self.outer_size, 2, 2, self.seq_size)
        self.strides = (4 * self.seq_size, 2 * self.seq_size, self.seq_size, 1)

    def digits(self):
        clip, seq = lax.axis_index("clip"), lax.axis_index("seq")
        return (clip // 4, (clip // 2) % 2, clip % 2, seq)

    def swap_outer(self, array, bit):
        flip = self.strides[OUTER] << bit
        return lax.ppermute(array, AXES, [(place, place ^ flip) for place in range(self.owners)])

    def outer_bits(self):
        return list(reversed(range(self.outer_size.bit_length() - 1)))

    def shift(self, array, axis, amount):
        size, stride = self.sizes[axis], self.strides[axis]
        pairs = []
        for place in range(self.owners):
            digit = (place // stride) % size
            pairs.append((place, place + ((digit + amount) % size - digit) * stride))
        return lax.ppermute(array, AXES, pairs)


OUTER, CROSS, CORE, SEQ = 0, 1, 2, 3


class Traffic:
    def __init__(self):
        self.active = []

    def add(self, stages):
        found = {}
        self.active.append([stages, next(stages), found])
        return found

    def tick(self, *state):
        flying = [entry[1] for entry in self.active]
        state, flying = lax.optimization_barrier((list(state), flying))
        going = []
        for (stages, _, found), arrays in zip(self.active, flying):
            try:
                going.append([stages, stages.send(arrays), found])
            except StopIteration as end:
                found["value"] = end.value
        self.active = going
        return state[0] if len(state) == 1 else state


def around(grid, array, axis):
    return [grid.shift(array, axis, amount) for amount in range(1, grid.sizes[axis])]


def join(pieces):
    return jnp.concatenate(pieces, axis=0)


def spread(steps, axis, size):
    return [
        step[:axis] + (amount,) + step[axis + 1 :] for amount in range(size) for step in steps
    ]


def place_kernel(grid, steps, splits, *refs):
    count = len(steps)
    pieces, outs, sem = refs[:count], refs[count : count + len(splits)], refs[-1]
    digits = grid.digits()
    copies = []
    for piece, found in zip(pieces, steps):
        for index, step in enumerate(found):
            place = 0
            for axis in range(4):
                size = grid.sizes[axis]
                place = place * size + lax.rem(digits[axis] + size - step[axis], size)
            for out, (start, stop, blocks) in zip(outs, splits):
                size = (stop - start) // blocks
                for block in range(blocks):
                    source = piece.at[index, :, pl.ds(start + block * size, size)]
                    target = out.at[place * blocks + block]
                    copies.append(pltpu.make_async_copy(source, target, sem.at[len(copies)]))
    for copy in copies:
        copy.start()
    for copy in copies:
        copy.wait()


def gather_rows(grid, shard, splits):
    rows, columns = shard.shape
    own = shard[None]
    own, *rounds = yield [own] + around(grid, own, OUTER)
    half = max(grid.outer_size // 2, 1)
    line = [(back, 0, 0, 0) for back in range(grid.outer_size)]
    groups = [[own] + rounds[: half - 1], rounds[half - 1 :]]
    steps = [line[:half], line[half:]]
    orders = [(CROSS, SEQ), (SEQ, CROSS)]
    pieces = [join(group) for group in groups]
    for turn in range(2):
        moved = [around(grid, piece, order[turn]) for piece, order in zip(pieces, orders)]
        pieces, moved = yield pieces, moved
        if turn == 0:
            pieces = [join([piece] + more) for piece, more in zip(pieces, moved)]
            steps = [
                spread(step, order[turn], grid.sizes[order[turn]])
                for step, order in zip(steps, orders)
            ]
    steps = [
        spread(step, order[1], grid.sizes[order[1]]) for step, order in zip(steps, orders)
    ]
    steps = [
        part[start : start + piece.shape[0]]
        for part, piece in zip(steps, pieces)
        for start in range(0, len(part), piece.shape[0])
    ]
    pieces = [part for piece, more in zip(pieces, moved) for part in [piece] + more]
    far = [grid.shift(piece, CORE, 1) for piece in pieces]
    steps = steps + [[step[:CORE] + (1,) + step[CORE + 1 :] for step in found] for found in steps]
    outs = pl.pallas_call(
        functools.partial(place_kernel, grid, steps, splits),
        out_shape=[
            jax.ShapeDtypeStruct(
                (grid.owners * blocks, rows, (stop - start) // blocks), shard.dtype
            )
            for start, stop, blocks in splits
        ],
        in_specs=[pl.BlockSpec(memory_space=pl.ANY)] * len(steps),
        out_specs=[pl.BlockSpec(memory_space=pltpu.VMEM)] * len(splits),
        scratch_shapes=[pltpu.SemaphoreType.DMA((grid.owners * sum(split[2] for split in splits),))],
        compiler_params=pltpu.CompilerParams(vmem_limit_bytes=VMEM_BYTES),
        cost_estimate=QUICK,
        name="place_rows",
    )(*pieces, *far)
    return [out.reshape(-1, out.shape[2]) for out in outs]


def exchange(grid, part, axis):
    size, digit = grid.sizes[axis], grid.digits()[axis]
    kept = lax.dynamic_slice_in_dim(part, digit, 1, axis)
    arrived = [
        grid.shift(lax.dynamic_slice_in_dim(part, (digit + amount) % size, 1, axis), axis, amount)
        for amount in range(1, size)
    ]
    return kept, arrived


def total_of(kept, arrived):
    return sum((piece.astype(jnp.float32) for piece in arrived), kept.astype(jnp.float32))


def by_core(grid, total):
    rows, columns = total.shape
    shape = grid.sizes + (rows // grid.owners, columns)
    core = grid.digits()[CORE]
    total = total.astype(jnp.bfloat16).reshape(shape)
    return [lax.dynamic_slice_in_dim(total, place, 1, CORE) for place in (core, 1 - core)]


def scatter_rows(grid, kept, sent, last=False):
    kept, arrived = yield kept, [grid.shift(sent, CORE, 1)]
    part = total_of(kept, arrived).astype(jnp.bfloat16)
    half = grid.outer_size // 2
    parts = [part[:half], part[half:]]
    orders = [(CROSS, SEQ), (SEQ, CROSS)]
    for turn in range(2):
        flying = yield [exchange(grid, part, order[turn]) for part, order in zip(parts, orders)]
        parts = [total_of(*entry).astype(jnp.bfloat16) for entry in flying]
    if last:
        kept, arrived = yield exchange(grid, join(parts), OUTER)
        return total_of(kept, arrived).reshape(kept.shape[-2:])
    outer = grid.digits()[OUTER]
    for bit in grid.outer_bits():
        upper = ((outer >> bit) & 1) == 1
        low, high = parts
        kept, sent = jnp.where(upper, high, low), jnp.where(upper, low, high)
        kept, arrived = yield kept, [grid.swap_outer(sent, bit)]
        part = total_of(kept, arrived)
        if bit:
            part = part.astype(jnp.bfloat16)
            half = part.shape[0] // 2
            parts = [part[:half], part[half:]]
    return part.reshape(part.shape[-2:])


def split_columns(rows_first, blocks):
    owners, rows, columns = rows_first.shape
    turned = rows_first.reshape(owners, blocks, rows // blocks, columns)
    return jnp.moveaxis(turned, 1, 2).reshape(owners * (rows // blocks), blocks * columns)


def turned_product(left, right):
    return lax.dot_general(
        left, right, (((0,), (0,)), ((), ())), preferred_element_type=jnp.float32
    )


def store_shares(pair, total, low, columns):
    first = lax.axis_index("clip") % 2 == 0
    for ref, here in zip(pair, (True, False)):
        part = jnp.where(first == here, total[:, :, 0], total[:, :, 1])
        part = part.reshape(-1, part.shape[-1]).astype(ref.dtype)
        ref[pl.ds(low, part.shape[0]), columns] = part


def up_shares_kernel(grid, normed_ref, before_ref, mixed_ref, branch_ref, kept, sent, turned):
    step, ups = pl.program_id(0), pl.num_programs(0) - 1
    outer, _, _, seq = grid.sizes
    width = normed_ref.shape[1]
    shape = (outer, 2, 2, seq * width // grid.owners, width)

    @pl.when(step == 0)
    def _():
        turned[...] = normed_ref[...].T

    @pl.when(step < ups)
    def _():
        total = times(turned[...], before_ref[...]).reshape(shape)
        store_shares((kept, sent), total, 0, slice(None))

    @pl.when(step == ups)
    def _():
        total = turned_product(mixed_ref[...], branch_ref[...]).reshape(shape)
        store_shares((kept, sent), total, 0, slice(None))


def up_shares(grid, normed, before, mixed, branch):
    frames, width = normed.shape
    blocks, rows = before.shape[1] // width, width // grid.owners
    if rows % 8:
        total = [outer_total(normed, before), outer_total(mixed, branch)]
        return by_core(grid, jnp.concatenate(total, axis=1))
    columns = before.shape[1] + width
    whole = pl.BlockSpec((frames, width), lambda i: (0, 0))
    half = pl.BlockSpec((width // 2, width), lambda i: (0, i))
    parts = pl.pallas_call(
        functools.partial(up_shares_kernel, grid),
        grid=(blocks + 1,),
        in_specs=[
            whole,
            pl.BlockSpec((frames, width), lambda i: (0, jnp.minimum(i, blocks - 1))),
            whole,
            whole,
        ],
        out_specs=[half, half],
        out_shape=[jax.ShapeDtypeStruct((width // 2, columns), jnp.bfloat16)] * 2,
        scratch_shapes=[pltpu.VMEM((width, frames), jnp.bfloat16)],
        compiler_params=pltpu.CompilerParams(vmem_limit_bytes=VMEM_BYTES),
        cost_estimate=QUICK,
        name="up_shares",
    )(normed, before, mixed, branch)
    shape = (grid.outer_size, 2, 1, grid.seq_size, rows, columns)
    return [part.reshape(shape) for part in parts]


def both_shares_kernel(
    grid, normed_ref, before_ref, mixed_ref, branch_ref, near_ref, far_ref, query_ref, pair_ref,
    pair_far_ref, kept, sent, turned, turned_far,
):
    step, ups = pl.program_id(0), pl.num_programs(0) - 4
    outer, _, _, seq = grid.sizes
    width = normed_ref.shape[1]
    shape = (outer, 2, 2, seq * width // grid.owners, width)

    @pl.when(step == 0)
    def _():
        turned[...] = normed_ref[...].T

    @pl.when(step < ups)
    def _():
        total = times(turned[...], before_ref[...]).reshape(shape)
        store_shares((kept, sent), total, 0, slice(None))

    @pl.when(step == ups)
    def _():
        total = turned_product(mixed_ref[...], branch_ref[...]).reshape(shape)
        store_shares((kept, sent), total, 0, slice(None))

    @pl.when(step == ups + 1)
    def _():
        turned[...] = near_ref[...].T
        turned_far[...] = far_ref[...].T
        total = times(turned[...], query_ref[...]).reshape(shape)
        store_shares((kept, sent), total, 0, slice(None))

    @pl.when(step > ups + 1)
    def _():
        total = times(turned[...], pair_ref[...]) + times(turned_far[...], pair_far_ref[...])
        store_shares((kept, sent), total.reshape(shape), 0, slice(None))


def both_shares(grid, normed, before, mixed, branch, near, far, query, pair, pair_far):
    frames, width = normed.shape
    blocks, rows = before.shape[1] // width, width // grid.owners
    if rows % 8:
        pairs = zip(
            up_shares(grid, normed, before, mixed, branch),
            mixing_shares(grid, near, far, query, pair, pair_far),
        )
        return [jnp.concatenate(pair, axis=-1) for pair in pairs]
    columns = before.shape[1] + 4 * width
    whole = pl.BlockSpec((frames, width), lambda i: (0, 0))
    half = pl.BlockSpec((width // 2, width), lambda i: (0, i))

    def late(i):
        return (0, jnp.maximum(i - blocks - 2, 0))

    parts = pl.pallas_call(
        functools.partial(both_shares_kernel, grid),
        grid=(blocks + 4,),
        in_specs=[
            whole,
            pl.BlockSpec((frames, width), lambda i: (0, jnp.minimum(i, blocks - 1))),
            whole,
            whole,
            whole,
            pl.BlockSpec(far.shape, lambda i: (0, 0)),
            whole,
            pl.BlockSpec((frames, width), late),
            pl.BlockSpec((far.shape[0], width), late),
        ],
        out_specs=[half, half],
        out_shape=[jax.ShapeDtypeStruct((width // 2, columns), jnp.bfloat16)] * 2,
        scratch_shapes=[
            pltpu.VMEM((width, frames), jnp.bfloat16),
            pltpu.VMEM((width, far.shape[0]), jnp.bfloat16),
        ],
        compiler_params=pltpu.CompilerParams(vmem_limit_bytes=VMEM_BYTES),
        cost_estimate=QUICK,
        name="both_shares",
    )(normed, before, mixed, branch, near, far, query, pair, pair_far)
    shape = (grid.outer_size, 2, 1, grid.seq_size, rows, columns)
    return [part.reshape(shape) for part in parts]


def low_shares_kernel(grid, rows, active_ref, down_ref, kept, sent):
    seq = grid.seq_size
    width = down_ref.shape[1]
    total = turned_product(active_ref[...], down_ref[...])
    blocks = total.shape[0] // (4 * seq * rows)
    total = total.reshape(1, 2, 2, seq, blocks, rows, width)
    for block in range(blocks):
        part = total[:, :, :, :, block].reshape(1, 2, 2, seq * rows, width)
        store_shares((kept, sent), part, 0, slice(block * width, (block + 1) * width))


def low_shares(grid, active, down):
    frames, width = down.shape
    units = active.shape[1]
    blocks, rows = units // width, width // grid.owners
    if rows % 8:
        total = outer_total(active, down).reshape(grid.owners, -1, width)
        return by_core(grid, split_columns(total, blocks))
    line = units // grid.outer_size
    half = pl.BlockSpec((width // (2 * grid.outer_size), units), lambda i: (i, 0))
    parts = pl.pallas_call(
        functools.partial(low_shares_kernel, grid, rows),
        grid=(grid.outer_size,),
        in_specs=[
            pl.BlockSpec((frames, line), lambda i: (0, i)),
            pl.BlockSpec((frames, width), lambda i: (0, 0)),
        ],
        out_specs=[half, half],
        out_shape=[jax.ShapeDtypeStruct((width // 2, units), jnp.bfloat16)] * 2,
        compiler_params=pltpu.CompilerParams(vmem_limit_bytes=VMEM_BYTES),
        cost_estimate=QUICK,
        name="low_shares",
    )(active, down)
    shape = (grid.outer_size, 2, 1, grid.seq_size, rows, units)
    return [part.reshape(shape) for part in parts]


def mixing_shares_kernel(
    grid, near_ref, far_ref, query_ref, pair_ref, pair_far_ref, kept, sent, turned, turned_far
):
    step = pl.program_id(0)
    outer, _, _, seq = grid.sizes
    width = near_ref.shape[1]
    shape = (outer, 2, 2, seq * width // grid.owners, width)

    @pl.when(step == 0)
    def _():
        turned[...] = near_ref[...].T
        turned_far[...] = far_ref[...].T
        total = times(turned[...], query_ref[...]).reshape(shape)
        store_shares((kept, sent), total, 0, slice(None))

    @pl.when(step > 0)
    def _():
        total = times(turned[...], pair_ref[...]) + times(turned_far[...], pair_far_ref[...])
        store_shares((kept, sent), total.reshape(shape), 0, slice(None))


def mixing_shares(grid, near, far, query, pair, pair_far):
    frames, width = near.shape
    rows = width // grid.owners
    if rows % 8:
        total = jnp.concatenate(
            [
                outer_total(near, query),
                outer_total(near, pair) + outer_total(far, pair_far),
            ],
            axis=1,
        )
        return by_core(grid, total)
    near_spec = pl.BlockSpec((frames, width), lambda i: (0, 0))
    half = pl.BlockSpec((width // 2, width), lambda i: (0, i))
    parts = pl.pallas_call(
        functools.partial(mixing_shares_kernel, grid),
        grid=(3,),
        in_specs=[
            near_spec,
            pl.BlockSpec(far.shape, lambda i: (0, 0)),
            near_spec,
            pl.BlockSpec((frames, width), lambda i: (0, jnp.maximum(i - 1, 0))),
            pl.BlockSpec((far.shape[0], width), lambda i: (0, jnp.maximum(i - 1, 0))),
        ],
        out_specs=[half, half],
        out_shape=[jax.ShapeDtypeStruct((width // 2, 3 * width), jnp.bfloat16)] * 2,
        scratch_shapes=[
            pltpu.VMEM((width, frames), jnp.bfloat16),
            pltpu.VMEM((width, far.shape[0]), jnp.bfloat16),
        ],
        compiler_params=pltpu.CompilerParams(vmem_limit_bytes=VMEM_BYTES),
        cost_estimate=QUICK,
        name="mixing_shares",
    )(near, far, query, pair, pair_far)
    shape = (grid.outer_size, 2, 1, grid.seq_size, rows, 3 * width)
    return [part.reshape(shape) for part in parts]


def head_of(array, head):
    lane = lax.broadcasted_iota(jnp.int32, array.shape, 1)
    inside = lane < HEAD_DIM if head == 0 else lane >= HEAD_DIM
    return jnp.where(inside, array, jnp.zeros_like(array))


def times_transposed(left, right):
    return lax.dot_general(
        left, right, (((1,), (1,)), ((), ())), preferred_element_type=jnp.float32
    )


def times(left, right):
    return lax.dot_general(
        left, right, (((1,), (0,)), ((), ())), preferred_element_type=jnp.float32
    )


def attend_kernel(q_ref, k_ref, v_ref, k_far_ref, v_far_ref, o_ref, log_ref):
    keys = (k_ref[...], k_far_ref[...])
    values = (v_ref[...].T, v_far_ref[...].T)
    query = q_ref[...]
    mixed, logs = [], []
    for head in range(2):
        rows = slice(head * HEAD_DIM, (head + 1) * HEAD_DIM)
        part = head_of(query, head)
        scores = [times_transposed(key, part) for key in keys]
        highest = functools.reduce(
            jnp.maximum, [jnp.max(score, axis=0, keepdims=True) for score in scores]
        )
        weights = [jnp.exp2((score - highest) * LOG2_SCALE) for score in scores]
        total = sum(jnp.sum(weight, axis=0, keepdims=True) for weight in weights)
        inverse = 1.0 / total
        probs = [(weight * inverse).astype(jnp.bfloat16) for weight in weights]
        mixed.append(sum(times(value[rows], prob) for value, prob in zip(values, probs)))
        logs.append(highest * LOG2_SCALE + jnp.log2(total))
    o_ref[...] = jnp.concatenate(mixed, axis=0).T.astype(o_ref.dtype)
    log_ref[0] = jnp.concatenate(logs, axis=0)


def attend_back_kernel(
    q_ref, k_ref, v_ref, k_far_ref, v_far_ref, log_ref, g_ref,
    dq_ref, d_ref, d_far_ref,
):
    width = q_ref.shape[1] * pl.num_programs(0)
    column = pl.multiple_of(pl.program_id(0) * 128, 128)
    second = pl.multiple_of(d_ref.shape[1] // 2 + pl.program_id(0) * 128, 128)
    keys = (k_ref[...], k_far_ref[...])
    keys_turned = [key.T for key in keys]
    values = (v_ref[...], v_far_ref[...])
    query, grad = q_ref[...], g_ref[...]
    scale = HEAD_DIM ** (-0.5)
    grad_query = []
    grad_keys, grad_values = [None, None], [None, None]
    for head in range(2):
        rows = slice(head * HEAD_DIM, (head + 1) * HEAD_DIM)
        part, grad_part = head_of(query, head), head_of(grad, head)
        log = log_ref[0, head : head + 1, :]
        probs = [
            jnp.exp2(times_transposed(key, part) * LOG2_SCALE - log) for key in keys
        ]
        pulls = [times_transposed(value, grad_part) for value in values]
        inner = sum(
            jnp.sum(prob * pull, axis=0, keepdims=True) for prob, pull in zip(probs, pulls)
        )
        scores = [
            (prob * (pull - inner)).astype(jnp.bfloat16) for prob, pull in zip(probs, pulls)
        ]
        grad_query.append(
            sum(times(key[rows], score) for key, score in zip(keys_turned, scores))
        )
        for side in range(2):
            more = times(scores[side], part)
            grad_keys[side] = more if head == 0 else grad_keys[side] + more
            more = times(probs[side].astype(jnp.bfloat16), grad_part)
            grad_values[side] = more if head == 0 else grad_values[side] + more
    dq_ref[...] = (jnp.concatenate(grad_query, axis=0).T * scale).astype(dq_ref.dtype)
    for side, out in enumerate((d_ref, d_far_ref)):
        out[:, pl.ds(column, 128)] = (grad_keys[side] * scale).astype(out.dtype)
        out[:, pl.ds(second, 128)] = grad_values[side].astype(out.dtype)


def block_specs(frames, far, blocks):
    return [
        pl.BlockSpec((frames, 128), lambda i: (0, i)),
        pl.BlockSpec((frames, 128), lambda i: (0, i)),
        pl.BlockSpec((frames, 128), lambda i: (0, i + blocks)),
        pl.BlockSpec((far, 128), lambda i: (0, i)),
        pl.BlockSpec((far, 128), lambda i: (0, i + blocks)),
    ]


def attend(query, pair, pair_far):
    frames, width = query.shape
    far, blocks = pair_far.shape[0], width // 128
    return pl.pallas_call(
        attend_kernel,
        grid=(blocks,),
        in_specs=block_specs(frames, far, blocks),
        out_specs=[
            pl.BlockSpec((frames, 128), lambda i: (0, i)),
            pl.BlockSpec((1, 2, frames), lambda i: (i, 0, 0)),
        ],
        out_shape=[
            jax.ShapeDtypeStruct((frames, width), jnp.bfloat16),
            jax.ShapeDtypeStruct((blocks, 2, frames), jnp.float32),
        ],
        compiler_params=pltpu.CompilerParams(vmem_limit_bytes=VMEM_BYTES),
        cost_estimate=QUICK,
        name="attend",
    )(query, pair, pair, pair_far, pair_far)


def attend_back(query, pair, pair_far, logs, grad):
    frames, width = query.shape
    far, blocks = pair_far.shape[0], width // 128
    return pl.pallas_call(
        attend_back_kernel,
        grid=(blocks,),
        in_specs=block_specs(frames, far, blocks)
        + [
            pl.BlockSpec((1, 2, frames), lambda i: (i, 0, 0)),
            pl.BlockSpec((frames, 128), lambda i: (0, i)),
        ],
        out_specs=[
            pl.BlockSpec((frames, 128), lambda i: (0, i)),
            pl.BlockSpec((frames, 2 * width), lambda i: (0, 0)),
            pl.BlockSpec((far, 2 * width), lambda i: (0, 0)),
        ],
        out_shape=[
            jax.ShapeDtypeStruct((frames, width), jnp.bfloat16),
            jax.ShapeDtypeStruct((frames, 2 * width), jnp.bfloat16),
            jax.ShapeDtypeStruct((far, 2 * width), jnp.bfloat16),
        ],
        compiler_params=pltpu.CompilerParams(vmem_limit_bytes=VMEM_BYTES),
        cost_estimate=QUICK,
        name="attend_back",
    )(query, pair, pair, pair_far, pair_far, logs, grad)


def normal_parts(rows):
    center = jnp.mean(rows, axis=-1, keepdims=True)
    spread = rows - center
    variance = jnp.mean(spread * spread, axis=-1, keepdims=True)
    rate = lax.rsqrt(variance + EPSILON)
    return spread * rate, rate


def normal_back(grad, rows, gain):
    unit, rate = normal_parts(rows)
    scaled = grad * gain
    pulled = rate * (
        scaled
        - jnp.mean(scaled, axis=-1, keepdims=True)
        - unit * jnp.mean(scaled * unit, axis=-1, keepdims=True)
    )
    return pulled, jnp.sum(grad * unit, axis=0), jnp.sum(grad, axis=0)


def raise_kernel(left_ref, right_ref, bias_ref, active_ref, slope_ref):
    values = times(left_ref[...], right_ref[...]) + bias_ref[...]
    below = 0.5 + 0.5 * lax.erf(values * math.sqrt(0.5))
    density = jnp.exp(-0.5 * values * values) * (1.0 / math.sqrt(2.0 * math.pi))
    active_ref[...] = (values * below).astype(active_ref.dtype)
    slope_ref[...] = below + values * density


def raise_width(left, right, bias):
    frames, width = left.shape
    units = right.shape[1]
    tile = 512
    return pl.pallas_call(
        raise_kernel,
        grid=(units // tile,),
        in_specs=[
            pl.BlockSpec((frames, width), lambda i: (0, 0)),
            pl.BlockSpec((width, tile), lambda i: (0, i)),
            pl.BlockSpec((1, tile), lambda i: (0, i)),
        ],
        out_specs=[pl.BlockSpec((frames, tile), lambda i: (0, i))] * 2,
        out_shape=[
            jax.ShapeDtypeStruct((frames, units), jnp.bfloat16),
            jax.ShapeDtypeStruct((frames, units), jnp.float32),
        ],
        compiler_params=pltpu.CompilerParams(vmem_limit_bytes=VMEM_BYTES),
        cost_estimate=QUICK,
        name="raise_width",
    )(left, right, bias.reshape(1, -1))


def outer_total(left, right):
    return lax.dot_general(
        left, right, (((0,), (0,)), ((), ())), preferred_element_type=jnp.float32
    )


def column_total(values):
    return jnp.sum(values.astype(jnp.float32), axis=0)


SMALL = (0, 1, 3, 5, 6, 7, 9, 11)


def everywhere(grid, array):
    for axis in (OUTER, CROSS, SEQ, CORE):
        array = sum(around(grid, array, axis), array)
    return array


def gather_small(grid, params):
    place = lax.axis_index("clip") * grid.seq_size + lax.axis_index("seq")
    lanes = []
    for slot in SMALL:
        shard = params[slot]
        empty = jnp.zeros((LAYERS, shard.shape[1] * grid.owners), jnp.float32)
        lanes.append(lax.dynamic_update_slice_in_dim(empty, shard, place * shard.shape[1], 1))
    packed = jnp.concatenate(lanes, axis=1).astype(jnp.bfloat16)
    whole = everywhere(grid, packed).astype(jnp.float32)
    found, offset = [[] for _ in range(LAYERS)], 0
    for lane in lanes:
        for layer in range(LAYERS):
            found[layer].append(whole[layer, offset : offset + lane.shape[1]])
        offset += lane.shape[1]
    return found


def scatter_small(grid, totals):
    place = lax.axis_index("clip") * grid.seq_size + lax.axis_index("seq")
    lengths = [total.shape[0] for total in totals[0]]
    starts = [sum(lengths[:index]) for index in range(len(lengths) + 1)]
    amount = starts[-1]
    whole = sum(
        jnp.pad(
            total,
            (
                layer * amount + starts[index],
                (LAYERS - layer) * amount - starts[index + 1],
            ),
        )
        for layer in range(LAYERS)
        for index, total in enumerate(totals[layer])
    )
    whole = sum(around(grid, whole, CORE), whole)
    whole, moved = yield whole, around(grid, whole, SEQ)
    whole = sum(moved, whole)
    whole, moved = yield whole, around(grid, whole, CROSS)
    whole = sum(moved, whole)
    for bit in grid.outer_bits():
        whole, moved = yield whole, grid.swap_outer(whole, bit)
        whole = whole + moved
    whole = whole.reshape(LAYERS, -1)
    pieces, offset = [], 0
    for total in totals[0]:
        amount = total.shape[0] // grid.owners
        pieces.append(
            lax.dynamic_slice_in_dim(whole, offset + place * amount, amount, 1)
        )
        offset += total.shape[0]
    return pieces


def pair_of(normed, w_pair, bias):
    return (times(normed, w_pair) + bias).astype(jnp.bfloat16)


def body(frames, cotangent, *params):
    grid, traffic = Grid(), Traffic()
    width = frames.shape[2]
    rows = frames.shape[0] * frames.shape[1]
    units = params[8].shape[2]
    blocks = units // width
    shards = []
    for layer in range(LAYERS):
        mixing, out, up, down = [
            params[slot][layer].astype(jnp.bfloat16) for slot in (2, 4, 8, 10)
        ]
        shards.append((mixing, jnp.concatenate([out, up, split_columns(down[None], blocks)], 1)))
    edges = [width, 3 * width, 4 * width, 4 * width + units, 4 * width + 2 * units]
    starts = [0] + edges[:-1]
    splits = [(start, stop, 1) for start, stop in zip(starts, edges)]
    splits[-1] = splits[-1][:2] + (blocks,)
    behind = [(start - edges[1], stop - edges[1], count) for start, stop, count in splits[2:]]

    def normal(hidden, gain, shift):
        normed = (normal_parts(hidden)[0] * gain + shift).astype(jnp.bfloat16)
        return normed, join(around(grid, normed, SEQ))

    hidden = frames.reshape(rows, width)
    kept = [{} for _ in range(LAYERS)]

    first = shards[0][0]
    first, vectors = lax.optimization_barrier((first, [params[slot] for slot in SMALL]))
    mixing = traffic.add(gather_rows(grid, first, tuple(splits[:2])))
    small = gather_small(grid, dict(zip(SMALL, vectors)))
    hidden = traffic.tick(hidden)
    rest = traffic.add(gather_rows(grid, shards[0][1], tuple(behind)))
    normed, normed_far = normal(hidden, *small[0][:2])
    last = [jnp.concatenate([shards[1][0], shards[1][1][:, : width + units]], axis=1),
            params[10][1].astype(jnp.bfloat16)]
    hidden, normed, normed_far, last = traffic.tick(hidden, normed, normed_far, last)
    wide, w_last = [lax.all_gather(part, AXES, axis=0, tiled=True) for part in last]
    second = {"value": [wide[:, start:stop] for start, stop, _ in splits[:-1]] + [w_last]}
    hidden, normed, normed_far = traffic.tick(hidden, normed, normed_far)
    for layer in range(LAYERS):
        g1, s1, bm, bo, g2, s2, bu, bd = small[layer]
        keep = kept[layer]
        if layer == 0:
            while "value" not in mixing:
                hidden, normed, normed_far = traffic.tick(hidden, normed, normed_far)
            w_query, w_pair = mixing["value"]
        else:
            while "value" not in second:
                hidden, normed, normed_far = traffic.tick(hidden, normed, normed_far)
            w_query, w_pair, w_out, w_up, w_down = second["value"]
        query = (times(normed, w_query) + bm[:width]).astype(jnp.bfloat16)
        pair_bias = jnp.concatenate([jnp.zeros((width,), jnp.float32), bm[width:]])
        pair, pair_far = [pair_of(part, w_pair, pair_bias) for part in (normed, normed_far)]
        attended, logs = attend(query, pair, pair_far)
        keep.update(
            hidden=hidden, normed=normed, normed_far=normed_far, query=query, pair=pair,
            pair_far=pair_far, logs=logs, w_query=w_query, w_pair=w_pair,
        )
        if layer == 0:
            while "value" not in rest:
                attended = traffic.tick(attended)
            w_out, w_up, w_down = rest["value"]
        middle = hidden + (times(attended, w_out) + bo)
        normed_two = (normal_parts(middle)[0] * g2 + s2).astype(jnp.bfloat16)
        active, slope = raise_width(normed_two, w_up, bu)
        keep.update(
            attended=attended, middle=middle, normed_two=normed_two, active=active,
            slope=slope, w_out=w_out, w_up=w_up, w_down=w_down,
        )
        hidden = middle + (times(active, w_down) + bd)
        if layer + 1 < LAYERS:
            normed, normed_far = normal(hidden, *small[layer + 1][:2])

    grad_hidden = cotangent.reshape(rows, width)
    shares, totals = [None] * LAYERS, [None] * LAYERS
    for layer in reversed(range(LAYERS)):
        g1, s1, bm, bo, g2, s2, bu, bd = small[layer]
        keep = kept[layer]
        grad_down = grad_hidden.astype(jnp.bfloat16)
        grad_before = (times_transposed(grad_down, keep["w_down"]) * keep["slope"]).astype(
            jnp.bfloat16
        )
        down_bias = column_total(grad_down)
        low = low_shares(grid, keep["active"], grad_down)
        if layer + 1 < LAYERS:
            low, grad_hidden, grad_before = traffic.tick(low, grad_hidden, grad_before)
            low_share = traffic.add(scatter_rows(grid, *low))
        up_bias = column_total(grad_before)
        grad_two = times_transposed(grad_before, keep["w_up"])
        pulled, gain_two, shift_two = normal_back(grad_two, keep["middle"], g2)
        grad_middle = grad_hidden + pulled
        grad_branch = grad_middle.astype(jnp.bfloat16)
        out_bias = column_total(grad_branch)
        grad_attended = times_transposed(grad_branch, keep["w_out"]).astype(jnp.bfloat16)
        operands = (keep["normed_two"], grad_before, keep["attended"], grad_branch)
        if layer + 1 < LAYERS:
            up = up_shares(grid, *operands)
            up, grad_middle, grad_attended = traffic.tick(up, grad_middle, grad_attended)
            up_share = traffic.add(scatter_rows(grid, *up))
        else:
            low, grad_middle, grad_attended = traffic.tick(low, grad_middle, grad_attended)
            low_share = traffic.add(scatter_rows(grid, *low))
        grad_query, grad_pair, grad_far = attend_back(
            keep["query"], keep["pair"], keep["pair_far"], keep["logs"], grad_attended
        )
        grad_query, grad_pair, grad_far, operands = traffic.tick(
            grad_query, grad_pair, grad_far, operands
        )
        far = times_transposed(grad_far, keep["w_pair"]).astype(jnp.bfloat16)
        arrived = [
            grid.shift(far[(amount - 1) * rows : amount * rows], SEQ, grid.seq_size - amount)
            for amount in range(1, grid.seq_size)
        ]
        far, grad_query, grad_pair, grad_far, operands = lax.optimization_barrier(
            (far, grad_query, grad_pair, grad_far, operands)
        )
        attention = (keep["normed"], keep["normed_far"], grad_query, grad_pair, grad_far)
        if layer + 1 == LAYERS:
            mixed = both_shares(grid, *operands, *attention)
        else:
            mixed = mixing_shares(grid, *attention)
        mixing_bias = jnp.concatenate(
            [
                column_total(grad_query),
                column_total(grad_pair[:, width:]) + column_total(grad_far[:, width:]),
            ]
        )
        grad_normed = times_transposed(grad_query, keep["w_query"]) + times_transposed(
            grad_pair, keep["w_pair"]
        )
        grad_normed = total_of(grad_normed, arrived)
        pulled, gain_one, shift_one = normal_back(grad_normed, keep["hidden"], g1)
        grad_hidden = grad_middle + pulled
        mixed, grad_hidden = traffic.tick(mixed, grad_hidden)
        mixed_share = traffic.add(scatter_rows(grid, *mixed, layer == 0))
        if layer + 1 == LAYERS:
            up_share = mixed_share
        shares[layer] = (mixed_share, up_share, low_share)
        totals[layer] = (
            gain_one, shift_one, mixing_bias, out_bias, gain_two, shift_two, up_bias, down_bias,
        )
    owned = traffic.add(scatter_small(grid, totals))
    while traffic.active:
        grad_hidden = traffic.tick(grad_hidden)
    stacked = dict(zip(SMALL, owned["value"]))
    values = [[share["value"] for share in layer] for layer in shares]
    stacked[2] = jnp.stack([value[0][:, -3 * width :] for value in values])
    stacked[4] = jnp.stack([value[1][:, units : units + width] for value in values])
    stacked[8] = jnp.stack([value[1][:, :units] for value in values])
    lows = [value[2].reshape(-1, blocks, width) for value in values]
    stacked[10] = jnp.stack([jnp.moveaxis(low, 1, 0).reshape(-1, width) for low in lows])
    return tuple(
        [hidden.reshape(frames.shape), grad_hidden.reshape(frames.shape)]
        + [stacked[slot] for slot in range(12)]
    )


def solution(mesh):
    vector, matrix = P(None, AXES), P(None, AXES, None)
    whole = P("clip", "seq", None)
    params = tuple(matrix if slot in (2, 4, 8, 10) else vector for slot in range(12))
    return jax.shard_map(
        body,
        mesh=mesh,
        in_specs=(whole, whole) + params,
        out_specs=(whole, whole) + params,
        check_vma=False,
    )
```
